32 devices in a mesh: section: 4 (over x, core), gx: 2 (over y), gy: 4 (over z).
Axes of the slice: x: 2, y: 2, z: 4, core: 2. Of those that a mesh axis runs over, the one named last changes fastest.
Arguments:
- voltage: float32 [8, 64, 1024], P(None, ('section', 'gx'), 'gy'), may hold values from -1.8 to 1.8
- capacity: float32 [8, 64, 1024], P(None, ('section', 'gx'), 'gy'), may hold values from 0.05 to 0.5
- node_class: int32 [8, 64, 1024], P(None, ('section', 'gx'), 'gy'), may hold values from 0 to 7
- via_sites: int32 [7, 64, 1024], P(None, ('section', 'gx'), 'gy'), may hold values 0 or 1
- ball_sites: int32 [64, 1024], P(('section', 'gx'), 'gy'), may hold values 0 or 1
- load_type: int32 [64, 1024], P(('section', 'gx'), 'gy'), may hold values from 0 to 15
- load_table: float32 [16, 5], replicated, may hold values from -4 to 4
Outputs:
- sections: float32 [5, 8, 64, 1024], P(None, None, ('section', 'gx'), 'gy')
- next_voltage: float32 [8, 64, 1024], P(None, ('section', 'gx'), 'gy')
The draws below stay inside these ranges and needn't reach their ends.
Inputs may be any that keep to these rules, and one draw needn't show every extreme that they name: `node_class`: index into the table of 8 conductances. `load_type`: row of load_table.
All inputs are finite; a program needn't handle non-finite values. No bound on the sum of `via_sites` or of `ball_sites` on one device may be relied on, other than what follows from the above.
Results may differ from the reference program's by a relative error of at most 0.0003.
Values sent between devices are 32-bit elements; how exact they have to be, the bound alone decides.
A program may use at most 128 MiB of HBM per device.

```python
import math
import jax
import jax.numpy as jnp
import numpy as np
from jax import lax

LAYERS = 8
SECTIONS = 5
LEVELS = 3
SWEEPS = 2
COARSE_SWEEPS = 4
CYCLES = 2
CLASSES = 8
LOADS = 16
NX = 64
NY = 1024


def place_ends(drawn, key, low, high):
    longest = drawn.shape.index(max(drawn.shape))
    spots = []
    for shift in (0, 1):
        where = [jax.random.randint(jax.random.fold_in(key, axis), (), 0, length) for axis, length in enumerate(drawn.shape)]
        where[longest] = (where[longest] + shift) % drawn.shape[longest]
        spots.append(tuple(where))
    return drawn.at[spots[0]].set(low).at[spots[1]].set(high)


def block_scale(own_key, dims, cuts, low, top_value):
    def one(position, parts):
        heights = jax.random.uniform(jax.random.fold_in(jax.random.fold_in(own_key, 6), position), (parts,), jnp.float32, low / len(cuts), top_value / len(cuts))
        return jnp.repeat(jnp.exp(heights), dims[position] // parts).reshape((-1,) + (1,) * (len(dims) - position - 1))

    gain = one(*cuts[0])
    for cut in cuts[1:]:
        gain = gain * one(*cut)
    return gain


def cumulative_ranks(count, slope):
    weights = [(1 << 20) // math.isqrt(grade ** slope) + 1 for grade in range(1, count + 1)]
    deviation = 1 + sum(weights) // (1 << 30)
    return np.cumsum(np.array([max(1, weight // deviation) for weight in weights]))


def ranked(stream_key, shape, amount, skew):
    grid = cumulative_ranks(amount, skew)
    ticket = jax.random.randint(jax.random.fold_in(stream_key, 1), shape, 0, int(grid[amount - 1]))
    grade = jnp.searchsorted(jnp.asarray(grid, jnp.int32), ticket, side="right")
    return jax.random.permutation(jax.random.fold_in(stream_key, 2), amount)[grade].astype(jnp.int32)


def normal_values(stream_key, shape, width, limit, split=(), dtype=jnp.bfloat16):
    values = jax.random.normal(stream_key, shape, jnp.float32) * width
    if len(split) > 0:
        values = block_scale(stream_key, shape, split, -0.22, 0.18) * values
    return jnp.clip(values, min=-limit, max=limit).astype(dtype)


def setup_inputs(seed: int = 0) -> dict:
    key_of = jax.random.split(jax.random.key(seed), 8)
    return {
        "voltage": normal_values(key_of[0], (LAYERS, NX, NY), 0.3, 1.8, ((1, 8), (2, 4)), jnp.float32),
        "capacity": jnp.clip(jnp.exp(math.log(0.5) - 2.3025851 * jax.random.uniform(key_of[1], (LAYERS, NX, NY), jnp.float32) ** block_scale(key_of[1], (LAYERS, NX, NY), ((1, 8), (2, 4)), -0.2, 0.2)), 0.05, 0.5),
        "node_class": place_ends(jax.random.randint(key_of[2], (LAYERS, NX, NY), 0, CLASSES), jax.random.fold_in(key_of[2], 1), 0, CLASSES - 1).astype(jnp.int32),
        "via_sites": place_ends((jax.random.randint(key_of[3], (LAYERS - 1, NX, NY), 0, 3) < 1).astype(jnp.int32), jax.random.fold_in(key_of[3], 1), 0, 1),
        "ball_sites": place_ends((jax.random.randint(key_of[4], (NX, NY), 0, 16) < 1).astype(jnp.int32), jax.random.fold_in(key_of[4], 1), 0, 1),
        "load_type": place_ends(ranked(key_of[5], (NX, NY), LOADS, 2), jax.random.fold_in(key_of[5], 3), 0, LOADS - 1).astype(jnp.int32),
        "load_table": normal_values(key_of[6], (LOADS, SECTIONS), 1.0, 4.0, (), jnp.float32),
    }


node_table = (0.35, 0.55, 0.8, 1.1, 1.5, 2.0, 2.7, 3.6)
via_conductance = 2.5
ball_conductance = 4.0
damping = 0.8
slab_partner = (0, 2, 1, 4, 3)


def pair_times(first, second):
    return (first[0] * second[0] - first[1] * second[1], first[0] * second[1] + first[1] * second[0])


def pair_over(first, second):
    divisor = second[0] * second[0] + second[1] * second[1]
    return ((first[0] * second[0] + first[1] * second[1]) / divisor,
            (first[1] * second[0] - first[0] * second[1]) / divisor)


def pair_minus(first, second):
    return (first[0] - second[0], first[1] - second[1])


def poly_value(coeffs, point):
    total = (0.0, 0.0)
    for c in reversed(coeffs):
        total = pair_times(total, point)
        total = (total[0] + c, total[1])
    return total


def poly_product(first, second):
    result = [0.0] * (len(first) + len(second) - 1)
    for i in range(len(first)):
        for j in range(len(second)):
            result[i + j] = result[i + j] + first[i] * second[j]
    return result


def poly_roots(coeffs):
    leading = coeffs[-1]
    scaled = [c / leading for c in coeffs]
    degree = len(coeffs) - 1
    guesses = []
    current = (1.0, 0.0)
    for k in range(degree):
        guesses.append(current)
        current = pair_times(current, (0.4, 0.9))
    for repeat_index in range(800):
        for k in range(degree):
            divisor = (1.0, 0.0)
            for j in range(degree):
                if j != k:
                    divisor = pair_times(divisor, pair_minus(guesses[k], guesses[j]))
            guesses[k] = pair_minus(guesses[k], pair_over(poly_value(scaled, guesses[k]), divisor))
    return guesses


def matrix_product(first, second):
    return [[sum(first[i][k] * second[k][j] for k in range(len(second))) for j in range(len(second[0]))]
            for i in range(len(first))]


def matrix_inverse(matrix):
    order = len(matrix)
    work = [list(matrix[i]) + [1.0 if i == j else 0.0 for j in range(order)] for i in range(order)]
    for column in range(order):
        pivot = column
        for i in range(column + 1, order):
            if abs(work[i][column]) > abs(work[pivot][column]):
                pivot = i
        work[column], work[pivot] = work[pivot], work[column]
        factor = work[column][column]
        work[column] = [entry / factor for entry in work[column]]
        for i in range(order):
            if i != column:
                scale_row = work[i][column]
                work[i] = [work[i][j] - scale_row * work[column][j] for j in range(2 * order)]
    return [row[order:] for row in work]


def eigen_vector(matrix, value):
    order = len(matrix)
    size_inner = order - 1
    system = []
    for i in range(size_inner):
        row = []
        for j in range(order):
            entry = (matrix[i][j], 0.0)
            if i == j:
                entry = pair_minus(entry, value)
            row.append(entry)
        row[order - 1] = (-row[order - 1][0], -row[order - 1][1])
        system.append(row)
    for column in range(size_inner):
        pivot = column
        for i in range(column + 1, size_inner):
            left_size = system[i][column][0] ** 2 + system[i][column][1] ** 2
            right_size = system[pivot][column][0] ** 2 + system[pivot][column][1] ** 2
            if left_size > right_size:
                pivot = i
        system[column], system[pivot] = system[pivot], system[column]
        for i in range(size_inner):
            if i != column:
                factor = pair_over(system[i][column], system[column][column])
                system[i] = [pair_minus(system[i][j], pair_times(factor, system[column][j])) for j in range(order)]
    vector = [pair_over(system[i][order - 1], system[i][i]) for i in range(size_inner)]
    vector.append((1.0, 0.0))
    return vector


def radau_tables():
    section_count = 5
    generator = [1.0]
    for k in range(section_count - 1):
        generator = poly_product(generator, [0.0, 1.0])
    for k in range(section_count):
        generator = poly_product(generator, [-1.0, 1.0])
    for k in range(section_count - 1):
        generator = [j * generator[j] for j in range(1, len(generator))]
    abscissae = sorted(root[0] for root in poly_roots(generator))
    vander = [[abscissae[i] ** j for j in range(section_count)] for i in range(section_count)]
    integrals = [[abscissae[i] ** (j + 1) / (j + 1) for j in range(section_count)] for i in range(section_count)]
    butcher = matrix_product(integrals, matrix_inverse(vander))
    inverse = matrix_inverse(butcher)
    coeffs = [0.0] * (section_count + 1)
    coeffs[section_count] = 1.0
    current = [[0.0] * section_count for _ in range(section_count)]
    for k in range(1, section_count + 1):
        current = matrix_product(inverse, current)
        for i in range(section_count):
            current[i][i] = current[i][i] + coeffs[section_count - k + 1]
        applied = matrix_product(inverse, current)
        coeffs[section_count - k] = -sum(applied[i][i] for i in range(section_count)) / k
    eigen_values = poly_roots(coeffs)
    real_pick = 0
    for k in range(section_count):
        if abs(eigen_values[k][1]) < abs(eigen_values[real_pick][1]):
            real_pick = k
    upper_half = [k for k in range(section_count) if eigen_values[k][1] > 1e-9]
    upper_half = sorted(upper_half, key=lambda k: -eigen_values[k][0])
    columns = [[entry[0] for entry in eigen_vector(inverse, (eigen_values[real_pick][0], 0.0))]]
    for k in upper_half:
        vector = eigen_vector(inverse, eigen_values[k])
        columns.append([entry[0] for entry in vector])
        columns.append([entry[1] for entry in vector])
    transform = [[columns[j][i] for j in range(section_count)] for i in range(section_count)]
    inverse_transform = matrix_inverse(transform)
    blocks = matrix_product(matrix_product(inverse_transform, inverse), transform)
    diagonal = [blocks[k][k] for k in range(section_count)]
    coupling = [blocks[k][slab_partner[k]] if slab_partner[k] != k else 0.0 for k in range(section_count)]
    return transform, inverse_transform, diagonal, coupling


def lookup(classes, values_table):
    result = jnp.zeros(classes.shape, jnp.float32)
    for k in range(len(values_table)):
        result = result + jnp.where(classes == k, jnp.float32(values_table[k]), jnp.float32(0.0))
    return result


def series(near_side, far_side):
    return 2.0 * near_side * far_side / (near_side + far_side)


def branch_set(conduct, padded, via_sites, ball_sites, capacity):
    lower_x = series(padded[:, :-2, 1:-1], conduct)
    upper_x = series(conduct, padded[:, 2:, 1:-1])
    lower_y = series(padded[:, 1:-1, :-2], conduct)
    upper_y = series(conduct, padded[:, 1:-1, 2:])
    vertical = jnp.where(via_sites == 1, jnp.float32(via_conductance), jnp.float32(0.0))
    ground = jnp.where(ball_sites == 1, jnp.float32(ball_conductance), jnp.float32(0.0))
    return (capacity, lower_x, upper_x, lower_y, upper_y, vertical, ground)


def layer_terms(vertical, ground, layers):
    zero_plane = jnp.zeros((1,) + vertical.shape[1:], jnp.float32)
    via_above = jnp.concatenate([vertical, zero_plane], axis=0)
    via_below = jnp.concatenate([zero_plane, vertical], axis=0)
    grounded = jnp.concatenate([ground[None], jnp.zeros((layers - 1,) + ground.shape, jnp.float32)], axis=0)
    return via_above, via_below, grounded


def network(voltage, padded_voltage, branches):
    capacity, lower_x, upper_x, lower_y, upper_y, vertical, ground = branches
    via_above, via_below, grounded = layer_terms(vertical, ground, voltage.shape[0])
    branch_total = lower_x + upper_x + lower_y + upper_y + via_above + via_below + grounded
    zero_plane = jnp.zeros((1,) + voltage.shape[1:], jnp.float32)
    volt_above = jnp.concatenate([voltage[1:], zero_plane], axis=0)
    volt_below = jnp.concatenate([zero_plane, voltage[:-1]], axis=0)
    inflow = (upper_x * padded_voltage[:, 2:, 1:-1] + lower_x * padded_voltage[:, :-2, 1:-1]
              + upper_y * padded_voltage[:, 1:-1, 2:] + lower_y * padded_voltage[:, 1:-1, :-2]
              + via_above * volt_above + via_below * volt_below)
    return branch_total * voltage - inflow


def section_sources(load_type, load_table):
    surface = jnp.zeros((SECTIONS,) + load_type.shape, jnp.float32)
    for t in range(LOADS):
        surface = surface + jnp.where((load_type == t)[None], load_table[t][:, None, None], jnp.float32(0.0))
    return surface


def pair_rows(array):
    extent = array.shape
    return array.reshape(extent[:-2] + (extent[-2] // 2, 2, extent[-1])).sum(axis=-2)


def pair_cols(array):
    extent = array.shape
    return array.reshape(extent[:-1] + (extent[-1] // 2, 2)).sum(axis=-1)


def take_rows(array, offset):
    extent = array.shape
    return array.reshape(extent[:-2] + (extent[-2] // 2, 2, extent[-1]))[..., offset, :]


def take_cols(array, offset):
    extent = array.shape
    return array.reshape(extent[:-1] + (extent[-1] // 2, 2))[..., offset]


def block_sum(array):
    return pair_cols(pair_rows(array))


def coarsen(branches):
    capacity, lower_x, upper_x, lower_y, upper_y, vertical, ground = branches
    return (block_sum(capacity), pair_cols(take_rows(lower_x, 0)), pair_cols(take_rows(upper_x, 1)),
            pair_rows(take_cols(lower_y, 0)), pair_rows(take_cols(upper_y, 1)),
            block_sum(vertical), block_sum(ground))


def level_operator(branches, shifts, couple, partner):
    capacity, lower_x, upper_x, lower_y, upper_y, vertical, ground = branches
    via_above, via_below, grounded = layer_terms(vertical, ground, capacity.shape[0])
    branch_total = lower_x + upper_x + lower_y + upper_y + via_above + via_below + grounded
    diagonal = shifts[:, None, None, None] * capacity + branch_total
    coupled = couple[:, None, None, None] * capacity
    diagonal_mate = jnp.stack([diagonal[p] for p in partner])
    coupled_mate = jnp.stack([coupled[p] for p in partner])
    determinant = diagonal * diagonal_mate - coupled * coupled_mate
    self_weight = diagonal_mate / determinant
    mate_weight = -coupled / determinant
    return (lower_x, upper_x, lower_y, upper_y, via_above, via_below, diagonal, coupled, self_weight, mate_weight, partner)


def operate(iterate, operator, neighbours):
    lower_x, upper_x, lower_y, upper_y, via_above, via_below, diagonal, coupled, self_weight, mate_weight, partner = operator
    upper_rows, lower_rows, right_cols, left_cols = neighbours
    zero_plane = jnp.zeros_like(iterate[:, :1])
    from_above = jnp.concatenate([iterate[:, 1:], zero_plane], axis=1)
    from_below = jnp.concatenate([zero_plane, iterate[:, :-1]], axis=1)
    inflow = (upper_x * upper_rows + lower_x * lower_rows + upper_y * right_cols + lower_y * left_cols
              + via_above * from_above + via_below * from_below)
    partner_field = jnp.stack([iterate[p] for p in partner])
    return diagonal * iterate - inflow + coupled * partner_field


def relax(iterate, source, operator, neighbour_fn):
    partner = operator[-1]
    if iterate is None:
        residual = source
    else:
        residual = source - operate(iterate, operator, neighbour_fn(iterate))
    mate_values = jnp.stack([residual[p] for p in partner])
    update = operator[8] * residual + operator[9] * mate_values
    if iterate is None:
        return damping * update
    return iterate + damping * update


def vcycle(operators, level_index, iterate, source, neighbour_fn):
    operator = operators[level_index]
    if level_index == len(operators) - 1:
        for _ in range(COARSE_SWEEPS):
            iterate = relax(iterate, source, operator, neighbour_fn)
        return iterate
    for _ in range(SWEEPS):
        iterate = relax(iterate, source, operator, neighbour_fn)
    residual = source - operate(iterate, operator, neighbour_fn(iterate))
    coarse = vcycle(operators, level_index + 1, None, block_sum(residual), neighbour_fn)
    iterate = iterate + jnp.repeat(jnp.repeat(coarse, 2, axis=2), 2, axis=3)
    for _ in range(SWEEPS):
        iterate = relax(iterate, source, operator, neighbour_fn)
    return iterate


def solve(source, branches, shifts, couple, partner, neighbour_fn):
    operators = []
    for level_index in range(LEVELS):
        if level_index > 0:
            branches = coarsen(branches)
        operators.append(level_operator(branches, shifts, couple, partner))
    iterate = vcycle(operators, 0, None, source, neighbour_fn)
    for _ in range(CYCLES - 1):
        iterate = vcycle(operators, 0, iterate, source, neighbour_fn)
    return iterate


def padded_faces(iterate):
    padded = jnp.pad(iterate, ((0, 0), (0, 0), (1, 1), (1, 1)))
    return padded[:, :, 2:, 1:-1], padded[:, :, :-2, 1:-1], padded[:, :, 1:-1, 2:], padded[:, :, 1:-1, :-2]


def reference(voltage, capacity, node_class, via_sites, ball_sites, load_type, load_table):
    transform, inverse_transform, diagonal_np, coupling_np = radau_tables()
    conduct = lookup(node_class, node_table)
    padded = jnp.pad(conduct, ((0, 0), (1, 1), (1, 1)))
    padded_voltage = jnp.pad(voltage, ((0, 0), (1, 1), (1, 1)))
    branches = branch_set(conduct, padded, via_sites, ball_sites, capacity)
    leakage = network(voltage, padded_voltage, branches)
    surface = section_sources(load_type, load_table)
    forcing = jnp.concatenate([jnp.broadcast_to(-leakage[:-1], (SECTIONS,) + leakage[:-1].shape),
                               (surface - leakage[-1])[:, None]], axis=1)
    transformed = jnp.einsum("jk,klrc->jlrc", jnp.asarray(inverse_transform, jnp.float32), forcing,
                             precision=lax.Precision.HIGHEST)
    shifts = jnp.asarray(diagonal_np, jnp.float32)
    couple = jnp.asarray(coupling_np, jnp.float32)
    solution = solve(transformed, branches, shifts, couple, slab_partner, padded_faces)
    sections = jnp.einsum("jk,klrc->jlrc", jnp.asarray(transform, jnp.float32), solution,
                        precision=lax.Precision.HIGHEST)
    return sections, voltage + sections[SECTIONS - 1]
```

```python
import functools

import jax
import jax.numpy as jnp
from jax import lax
from jax.experimental import pallas as pl
from jax.experimental.pallas import tpu as pltpu
from jax.sharding import PartitionSpec as P

SECTIONS = 5
LEVELS = 3
LOADS = 16
LANES = 128
ONE_CYCLE = 28
BOTH_CYCLES = 56

node_table = (0.35, 0.55, 0.8, 1.1, 1.5, 2.0, 2.7, 3.6)
via_conductance = 2.5
ball_conductance = 4.0
damping = 0.8
slab_partner = (0, 2, 1, 4, 3)
row_axes = ("section", "gx")


def pair_times(first, second):
    return (
        first[0] * second[0] - first[1] * second[1],
        first[0] * second[1] + first[1] * second[0],
    )


def pair_over(first, second):
    divisor = second[0] * second[0] + second[1] * second[1]
    return (
        (first[0] * second[0] + first[1] * second[1]) / divisor,
        (first[1] * second[0] - first[0] * second[1]) / divisor,
    )


def pair_minus(first, second):
    return (first[0] - second[0], first[1] - second[1])


def poly_value(coeffs, point):
    total = (0.0, 0.0)
    for c in reversed(coeffs):
        total = pair_times(total, point)
        total = (total[0] + c, total[1])
    return total


def poly_product(first, second):
    result = [0.0] * (len(first) + len(second) - 1)
    for i in range(len(first)):
        for j in range(len(second)):
            result[i + j] = result[i + j] + first[i] * second[j]
    return result


def poly_roots(coeffs):
    leading = coeffs[-1]
    scaled = [c / leading for c in coeffs]
    degree = len(coeffs) - 1
    guesses = []
    current = (1.0, 0.0)
    for k in range(degree):
        guesses.append(current)
        current = pair_times(current, (0.4, 0.9))
    for repeat_index in range(800):
        for k in range(degree):
            divisor = (1.0, 0.0)
            for j in range(degree):
                if j != k:
                    divisor = pair_times(divisor, pair_minus(guesses[k], guesses[j]))
            guesses[k] = pair_minus(guesses[k], pair_over(poly_value(scaled, guesses[k]), divisor))
    return guesses


def matrix_product(first, second):
    return [
        [
            sum((first[i][k] * second[k][j] for k in range(len(second))))
            for j in range(len(second[0]))
        ]
        for i in range(len(first))
    ]


def matrix_inverse(matrix):
    order = len(matrix)
    work = [list(matrix[i]) + [1.0 if i == j else 0.0 for j in range(order)] for i in range(order)]
    for column in range(order):
        pivot = column
        for i in range(column + 1, order):
            if abs(work[i][column]) > abs(work[pivot][column]):
                pivot = i
        work[column], work[pivot] = (work[pivot], work[column])
        factor = work[column][column]
        work[column] = [entry / factor for entry in work[column]]
        for i in range(order):
            if i != column:
                scale_row = work[i][column]
                work[i] = [work[i][j] - scale_row * work[column][j] for j in range(2 * order)]
    return [row[order:] for row in work]


def eigen_vector(matrix, value):
    order = len(matrix)
    size_inner = order - 1
    system = []
    for i in range(size_inner):
        row = []
        for j in range(order):
            entry = (matrix[i][j], 0.0)
            if i == j:
                entry = pair_minus(entry, value)
            row.append(entry)
        row[order - 1] = (-row[order - 1][0], -row[order - 1][1])
        system.append(row)
    for column in range(size_inner):
        pivot = column
        for i in range(column + 1, size_inner):
            left_size = system[i][column][0] ** 2 + system[i][column][1] ** 2
            right_size = system[pivot][column][0] ** 2 + system[pivot][column][1] ** 2
            if left_size > right_size:
                pivot = i
        system[column], system[pivot] = (system[pivot], system[column])
        for i in range(size_inner):
            if i != column:
                factor = pair_over(system[i][column], system[column][column])
                system[i] = [
                    pair_minus(system[i][j], pair_times(factor, system[column][j]))
                    for j in range(order)
                ]
    vector = [pair_over(system[i][order - 1], system[i][i]) for i in range(size_inner)]
    vector.append((1.0, 0.0))
    return vector


def radau_tables():
    section_count = 5
    generator = [1.0]
    for k in range(section_count - 1):
        generator = poly_product(generator, [0.0, 1.0])
    for k in range(section_count):
        generator = poly_product(generator, [-1.0, 1.0])
    for k in range(section_count - 1):
        generator = [j * generator[j] for j in range(1, len(generator))]
    abscissae = sorted((root[0] for root in poly_roots(generator)))
    vander = [[abscissae[i] ** j for j in range(section_count)] for i in range(section_count)]
    integrals = [
        [abscissae[i] ** (j + 1) / (j + 1) for j in range(section_count)]
        for i in range(section_count)
    ]
    butcher = matrix_product(integrals, matrix_inverse(vander))
    inverse = matrix_inverse(butcher)
    coeffs = [0.0] * (section_count + 1)
    coeffs[section_count] = 1.0
    current = [[0.0] * section_count for _ in range(section_count)]
    for k in range(1, section_count + 1):
        current = matrix_product(inverse, current)
        for i in range(section_count):
            current[i][i] = current[i][i] + coeffs[section_count - k + 1]
        applied = matrix_product(inverse, current)
        coeffs[section_count - k] = -sum((applied[i][i] for i in range(section_count))) / k
    eigen_values = poly_roots(coeffs)
    real_pick = 0
    for k in range(section_count):
        if abs(eigen_values[k][1]) < abs(eigen_values[real_pick][1]):
            real_pick = k
    upper_half = [k for k in range(section_count) if eigen_values[k][1] > 1e-09]
    upper_half = sorted(upper_half, key=lambda k: -eigen_values[k][0])
    columns = [[entry[0] for entry in eigen_vector(inverse, (eigen_values[real_pick][0], 0.0))]]
    for k in upper_half:
        vector = eigen_vector(inverse, eigen_values[k])
        columns.append([entry[0] for entry in vector])
        columns.append([entry[1] for entry in vector])
    transform = [[columns[j][i] for j in range(section_count)] for i in range(section_count)]
    inverse_transform = matrix_inverse(transform)
    blocks = matrix_product(matrix_product(inverse_transform, inverse), transform)
    diagonal = [blocks[k][k] for k in range(section_count)]
    coupling = [
        blocks[k][slab_partner[k]] if slab_partner[k] != k else 0.0 for k in range(section_count)
    ]
    return (transform, inverse_transform, diagonal, coupling)


def lookup(classes, values_table):
    result = jnp.zeros(classes.shape, jnp.float32)
    for k in range(len(values_table)):
        result = result + jnp.where(classes == k, jnp.float32(values_table[k]), jnp.float32(0.0))
    return result


def series(near_side, far_side):
    return 2.0 * near_side * far_side / (near_side + far_side)


def left_by(value, count):
    return pltpu.roll(value, LANES - count, axis=1)


def right_by(value, count):
    return pltpu.roll(value, count, axis=1)


def from_above(value):
    return pltpu.roll(value, value.shape[0] - 1, axis=0)


def from_below(value):
    return pltpu.roll(value, 1, axis=0)


def lane_ids(layers):
    return lax.broadcasted_iota(jnp.int32, (layers, LANES), 1)


def layer_ids(layers):
    return lax.broadcasted_iota(jnp.int32, (layers, LANES), 0)


def flux(here, ahead, behind_flux, gx, gy, gv, stride):
    along_x = gx * (ahead - here)
    along_y = gy * (left_by(here, stride) - here)
    along_z = gv * (from_above(here) - here)
    total = (
        (along_x - behind_flux)
        + (along_y - right_by(along_y, stride))
        + (along_z - from_below(along_z))
    )
    return along_x, total


def group_lanes(value, stride, low_half):
    return value + jnp.where(low_half, left_by(value, stride), right_by(value, stride))


def weights(cap, total, lam0, alpha, beta):
    real = lam0 * cap + total
    mate = beta * cap
    both = alpha * cap + total
    scale = damping / (both * both + mate * mate)
    return damping / real, both * scale, mate * scale


def correct(residual, sw0, sw, mw):
    return (
        sw0 * residual[0],
        sw * residual[1] - mw * residual[2],
        sw * residual[2] + mw * residual[1],
    )


def sweep(level, refs, scal, add=None, coarse=None):
    lam0, alpha, beta = scal
    g, x_ref, f_ref = refs[level]
    rows = g.shape[1]
    layers = g.shape[2]
    stride = 2**level
    step = min(4, rows)
    zero = jnp.zeros((layers, LANES), jnp.float32)

    def value(k, base, half, r):
        loaded = x_ref[k, base + r]
        if add is not None:
            loaded = loaded + add[k, half + r // 2]
        return loaded

    def body(b, carry):
        behind = list(carry[:3])
        xs = [[carry[3 + k]] for k in range(3)]
        base = b * step
        half = b * (step // 2)
        for k in range(3):
            for r in range(1, step + 1):
                xs[k].append(value(k, base, half, r))
        results = []
        for r in range(step):
            i = base + r
            gx, gy, gv = g[0, i], g[1, i], g[2, i]
            ground, cap = g[3, i], g[4, i]
            local = (lam0 * cap + ground, alpha * cap + ground)
            mate = beta * cap
            x0, x1, x2 = xs[0][r], xs[1][r], xs[2][r]
            pulled = []
            for k in range(3):
                behind[k], total = flux(xs[k][r], xs[k][r + 1], behind[k], gx, gy, gv, stride)
                pulled.append(total)
            residual = (
                f_ref[0, i] - local[0] * x0 + pulled[0],
                f_ref[1, i] - local[1] * x1 - mate * x2 + pulled[1],
                f_ref[2, i] - local[1] * x2 + mate * x1 + pulled[2],
            )
            if coarse is None:
                change = correct(residual, g[5, i], g[6, i], g[7, i])
                results.append([xs[k][r] + change[k] for k in range(3)])
            else:
                results.append(residual)
        if coarse is None:
            for r in range(step):
                for k in range(3):
                    x_ref[k, base + r] = results[r][k]
        else:
            g_next, x_next, f_next = refs[level + 1]
            low_half = (lane_ids(layers) // stride) % 2 == 0
            for r in range(0, step, 2):
                i = half + r // 2
                summed = [
                    group_lanes(results[r][k] + results[r + 1][k], stride, low_half)
                    for k in range(3)
                ]
                first = correct(summed, g_next[5, i], g_next[6, i], g_next[7, i])
                for k in range(3):
                    f_next[k, i] = summed[k]
                    x_next[k, i] = first[k]
        return tuple(behind) + tuple(xs[k][step] for k in range(3))

    init = (zero,) * 3 + tuple(value(k, 0, 0, 0) for k in range(3))
    lax.fori_loop(0, rows // step, body, init)


def coarsen(level, refs, scal):
    g = refs[level][0]
    g_next = refs[level + 1][0]
    layers = g.shape[2]
    stride = 2**level
    rows = g_next.shape[1]
    step = min(4, rows)

    def body(b, behind):
        low_half = (lane_ids(layers) // stride) % 2 == 0
        for r in range(step):
            i = b * step + r
            j = 2 * b * step + 2 * r
            gx = group_lanes(g[0, j + 1], stride, low_half)
            crossing = g[1, j] + g[1, j + 1]
            gy = jnp.where(low_half, left_by(crossing, stride), crossing)
            gv = group_lanes(g[2, j] + g[2, j + 1], stride, low_half)
            ground = group_lanes(g[3, j] + g[3, j + 1], stride, low_half)
            cap = group_lanes(g[4, j] + g[4, j + 1], stride, low_half)
            total = gx + behind + gy + right_by(gy, 2 * stride) + gv + from_below(gv) + ground
            found = weights(cap, total, *scal)
            for k, entry in enumerate((gx, gy, gv, ground, cap) + found):
                g_next[k, i] = entry
            behind = gx
        return behind

    lax.fori_loop(0, rows // step, body, jnp.zeros((layers, LANES), jnp.float32))


def cycle(refs, scal):
    sweep(0, refs, scal)
    sweep(0, refs, scal, coarse=True)
    sweep(1, refs, scal)
    sweep(1, refs, scal, coarse=True)
    for _ in range(3):
        sweep(2, refs, scal)
    sweep(1, refs, scal, add=refs[2][1])
    sweep(1, refs, scal)
    sweep(0, refs, scal, add=refs[1][1])
    sweep(0, refs, scal)


def kernel(
    sizes, transform, params, send, voltage, sections, next_voltage,
    recv, surf, g0, g1, g2, x0, x1, x2, f0, f1, f2, packed, landed, out_buf, out_recv,
    send_sem, recv_sem, ring_send, ring_recv, out_send, out_recv_sem, own_sem,
):
    parts, gx_count, gy_count, width, margin, columns = sizes
    layers = voltage.shape[0]
    block = voltage.shape[1]
    rows = parts * block
    regions = parts // 2
    mine = lax.axis_index("section") * gx_count + lax.axis_index("gx")
    gy_here = lax.axis_index("gy")
    system = mine % 2
    region = gy_here * regions + mine // 2
    all_regions = regions * gy_count

    def group_device(index):
        return {"section": index // gx_count, "gx": index % gx_count}

    def region_device(index):
        place = (index % regions) * 2 + system
        return {
            "section": place // gx_count,
            "gx": place % gx_count,
            "gy": index // regions,
        }

    after = region_device((region + 1) % all_regions)
    before = region_device((region + all_regions - 1) % all_regions)

    barrier = pltpu.get_barrier_semaphore()
    for d in range(1, parts):
        pl.semaphore_signal(
            barrier,
            inc=1,
            device_id=group_device((mine + d) % parts),
            device_id_type=pl.DeviceIdType.MESH,
        )
    for place in (after, before):
        pl.semaphore_signal(
            barrier, inc=1, device_id=place, device_id_type=pl.DeviceIdType.MESH
        )
    pl.semaphore_wait(barrier, parts + 1)

    copies = []
    for d in range(1, parts):
        peer = (mine + d) % parts
        copy = pltpu.make_async_remote_copy(
            src_ref=send.at[peer // 2],
            dst_ref=recv.at[mine],
            send_sem=send_sem.at[d],
            recv_sem=recv_sem.at[d],
            device_id=group_device(peer),
            device_id_type=pl.DeviceIdType.MESH,
        )
        copy.start()
        copies.append(copy)
    own = pltpu.make_async_copy(send.at[mine // 2], recv.at[mine], own_sem)
    own.start()
    lam0, alpha, beta = params[0], params[1], params[2]
    shares = (params[3], params[4], params[5])
    scal = (lam0, alpha, beta)
    zero = jnp.zeros((layers, LANES), jnp.float32)
    for x_ref in (x0, x1, x2):
        for k in range(3):
            x_ref[k, x_ref.shape[1] - 1] = zero
    own.wait()
    for copy in copies:
        copy.wait()

    def loads(b, carry):
        kind = recv[b, 4 * block]
        sums = [zero, zero, zero]
        for t in range(LOADS):
            here = kind == float(t)
            for k in range(3):
                sums[k] = jnp.where(here, params[6 + 3 * t + k], sums[k])
        for k in range(3):
            surf[k, b] = sums[k]
        return carry

    lax.fori_loop(0, parts, loads, 0)

    lanes = lane_ids(layers)
    level_of = layer_ids(layers)
    column = region * width - margin + lanes
    inside = (column >= 0) & (column < columns)
    joined = inside & (column < columns - 1) & (lanes < LANES - 1)

    def fine(b, carry):
        behind_gx, behind_flux = carry
        following = jnp.minimum(b + 1, parts - 1)
        for r in range(block):
            i = b * block + r
            volt, cap = recv[b, 4 * r], recv[b, 4 * r + 1]
            conduct = jnp.where(inside, recv[b, 4 * r + 2], 1.0)
            sites = recv[b, 4 * r + 3]
            if r + 1 < block:
                volt_ahead, conduct_ahead = recv[b, 4 * r + 4], recv[b, 4 * r + 6]
            else:
                volt_ahead, conduct_ahead = recv[following, 0], recv[following, 2]
            conduct_ahead = jnp.where(inside, conduct_ahead, 1.0)
            gx = series(conduct, conduct_ahead)
            if r + 1 == block:
                gx = gx * (b < parts - 1).astype(jnp.float32)
            gy = jnp.where(joined, series(conduct, left_by(conduct, 1)), 0.0)
            gv = jnp.where(level_of < layers - 1, sites, 0.0)
            ground = jnp.where(level_of == 0, from_below(sites), 0.0)
            total = gx + behind_gx + gy + right_by(gy, 1) + gv + from_below(gv) + ground
            found = weights(cap, total, *scal)
            behind_flux, pulled = flux(volt, volt_ahead, behind_flux, gx, gy, gv, 1)
            leak = ground * volt - pulled
            for k, entry in enumerate((gx, gy, gv, ground, cap) + found):
                g0[k, i] = entry
            source = [
                jnp.where(
                    level_of == layers - 1,
                    jnp.broadcast_to(surf[k, b, r : r + 1, :], (layers, LANES)),
                    0.0,
                )
                - shares[k] * leak
                for k in range(3)
            ]
            first = correct(source, *found)
            for k in range(3):
                f0[k, i] = source[k]
                x0[k, i] = first[k]
            behind_gx = gx
        return behind_gx, behind_flux

    lax.fori_loop(0, parts, fine, (zero, zero))
    refs = ((g0, x0, f0), (g1, x1, f1), (g2, x2, f2))
    coarsen(0, refs, scal)
    coarsen(1, refs, scal)
    cycle(refs, scal)

    if margin < BOTH_CYCLES:
        share = LANES // margin
        groups = rows // share

        def pack(q, carry):
            for side, begin in ((0, width), (1, margin)):
                for k in range(3):
                    joint = zero
                    for t in range(share):
                        turn = (margin * t - begin) % LANES
                        moved = x0[k, q + groups * t]
                        if turn:
                            moved = right_by(moved, turn)
                        joint = jnp.where(lanes // margin == t, moved, joint)
                    packed[side, k, q] = joint
            return carry

        lax.fori_loop(0, groups, pack, 0)
        ring = []
        for side, place in ((0, after), (1, before)):
            copy = pltpu.make_async_remote_copy(
                src_ref=packed.at[side],
                dst_ref=landed.at[side],
                send_sem=ring_send.at[side],
                recv_sem=ring_recv.at[side],
                device_id=place,
                device_id_type=pl.DeviceIdType.MESH,
            )
            copy.start()
            ring.append(copy)
        for copy in ring:
            copy.wait()

        def unpack(q, carry):
            for k in range(3):
                low = landed[0, k, q]
                high = landed[1, k, q]
                for t in range(share):
                    turn_low = (-margin * t) % LANES
                    turn_high = (margin + width - margin * t) % LANES
                    a = right_by(low, turn_low) if turn_low else low
                    c = right_by(high, turn_high) if turn_high else high
                    x = x0[k, q + groups * t]
                    x = jnp.where(lanes < margin, a, jnp.where(lanes < margin + width, x, c))
                    x0[k, q + groups * t] = x
            return carry

        lax.fori_loop(0, groups, unpack, 0)

    sweep(0, refs, scal)
    cycle(refs, scal)

    share = LANES // width
    groups = block // share
    copies = []
    for d in range(parts):
        peer = (mine + d) % parts
        for k in range(3):
            for q in range(groups):
                joint = zero
                for t in range(share):
                    turn = (width * t - margin) % LANES
                    moved = x0[k, peer * block + q + groups * t]
                    if turn:
                        moved = right_by(moved, turn)
                    joint = jnp.where(lanes // width == t, moved, joint)
                out_buf[d, k * groups + q] = joint
        if d == 0:
            own = pltpu.make_async_copy(out_buf.at[0], out_recv.at[mine], own_sem)
            own.start()
            continue
        copy = pltpu.make_async_remote_copy(
            src_ref=out_buf.at[d],
            dst_ref=out_recv.at[mine],
            send_sem=out_send.at[d],
            recv_sem=out_recv_sem.at[d],
            device_id=group_device(peer),
            device_id_type=pl.DeviceIdType.MESH,
        )
        copy.start()
        copies.append(copy)
    own.wait()
    for copy in copies:
        copy.wait()

    for tile in range(regions // share):
        mixed = [[None] * block for _ in range(SECTIONS)]
        for q in range(groups):
            fields = []
            for n in range(share):
                first = 2 * (tile * share + n)
                fields.append(
                    [out_recv[first, k * groups + q] for k in range(3)]
                    + [out_recv[first + 1, k * groups + q] for k in (1, 2)]
                )
            for s in range(SECTIONS):
                sums = [
                    sum(transform[s][k] * fields[n][k] for k in range(SECTIONS))
                    for n in range(share)
                ]
                for t in range(share):
                    joint = zero
                    for n in range(share):
                        turn = (width * (n - t)) % LANES
                        moved = right_by(sums[n], turn) if turn else sums[n]
                        joint = jnp.where(lanes // width == n, moved, joint)
                    mixed[s][q + groups * t] = joint
        place = pl.ds(tile * LANES, LANES)
        for s in range(SECTIONS):
            turned = jnp.swapaxes(jnp.stack(mixed[s]), 0, 1)
            sections[s, :, :, place] = turned
            if s == SECTIONS - 1:
                next_voltage[:, :, place] = voltage[:, :, place] + turned


def local(voltage, capacity, node_class, via_sites, ball_sites, load_type, load_table):
    transform, inverse_transform, diagonal, coupling = radau_tables()
    layers, block, wide = voltage.shape
    gx_count = lax.axis_size("gx")
    gy_count = lax.axis_size("gy")
    parts = lax.axis_size("section") * gx_count
    regions = parts // 2
    width = wide // regions
    margin = (LANES - width) // 2
    sizes = (parts, gx_count, gy_count, width, margin, wide * gy_count)
    rows = parts * block

    conduct = lookup(node_class, node_table)
    sites = jnp.concatenate(
        [
            jnp.where(via_sites == 1, jnp.float32(via_conductance), jnp.float32(0.0)),
            jnp.where(ball_sites == 1, jnp.float32(ball_conductance), jnp.float32(0.0))[None],
        ],
        axis=0,
    )
    planes = jnp.stack([voltage, capacity, conduct, sites]).transpose(2, 0, 1, 3)
    planes = planes.reshape(4 * block, layers, wide)
    planes = jnp.concatenate([planes, load_type.astype(jnp.float32)[None]], axis=0)
    forward = [(i, i + 1) for i in range(gy_count - 1)]
    backward = [(i + 1, i) for i in range(gy_count - 1)]
    low = lax.ppermute(planes[..., wide - margin :], "gy", forward)
    high = lax.ppermute(planes[..., :margin], "gy", backward)
    planes = jnp.concatenate([low, planes, high], axis=-1)
    send = jnp.stack([planes[..., width * k : width * k + LANES] for k in range(regions)])

    mine = lax.axis_index("section") * gx_count + lax.axis_index("gx")
    leading = mine % 2 == 0

    def chosen(table):
        first = [table[0], table[1], table[2]]
        second = [table[0], table[3], table[4]]
        return jnp.where(
            leading, jnp.asarray(first, jnp.float32), jnp.asarray(second, jnp.float32)
        )

    mixing = chosen(inverse_transform)
    shifts = chosen(diagonal)
    couple = chosen(coupling)
    currents = jnp.sum(load_table[:, None, :] * mixing[None], axis=-1)
    params = jnp.concatenate(
        [shifts[:2], couple[1:2], jnp.sum(mixing, axis=1), currents.reshape(-1)]
    )

    def vmem(*shape):
        return pltpu.VMEM(shape, jnp.float32)

    def levels(count, extra):
        return [vmem(count, rows // 2**m + extra, layers, LANES) for m in range(LEVELS)]

    mid = rows * margin // LANES if margin < BOTH_CYCLES else 1
    back = 3 * block * width // LANES
    return pl.pallas_call(
        functools.partial(kernel, sizes, transform),
        out_shape=(
            jax.ShapeDtypeStruct((SECTIONS, layers, block, wide), jnp.float32),
            jax.ShapeDtypeStruct((layers, block, wide), jnp.float32),
        ),
        in_specs=[
            pl.BlockSpec(memory_space=pltpu.SMEM),
            pl.BlockSpec(memory_space=pltpu.VMEM),
            pl.BlockSpec(memory_space=pltpu.VMEM),
        ],
        out_specs=(
            pl.BlockSpec(memory_space=pltpu.VMEM),
            pl.BlockSpec(memory_space=pltpu.VMEM),
        ),
        scratch_shapes=[
            vmem(parts, 4 * block + 1, layers, LANES),
            vmem(3, parts, block, LANES),
            *levels(8, 0),
            *levels(3, 1),
            *levels(3, 0),
            vmem(2, 3, mid, layers, LANES),
            vmem(2, 3, mid, layers, LANES),
            vmem(parts, back, layers, LANES),
            vmem(parts, back, layers, LANES),
            pltpu.SemaphoreType.DMA((parts,)),
            pltpu.SemaphoreType.DMA((parts,)),
            pltpu.SemaphoreType.DMA((2,)),
            pltpu.SemaphoreType.DMA((2,)),
            pltpu.SemaphoreType.DMA((parts,)),
            pltpu.SemaphoreType.DMA((parts,)),
            pltpu.SemaphoreType.DMA,
        ],
        compiler_params=pltpu.CompilerParams(
            collective_id=0, has_side_effects=True, vmem_limit_bytes=60 * 1024 * 1024
        ),
    )(params, send, voltage)


def solution(mesh):
    return jax.shard_map(
        local,
        mesh=mesh,
        in_specs=(
            P(None, row_axes, "gy"),
            P(None, row_axes, "gy"),
            P(None, row_axes, "gy"),
            P(None, row_axes, "gy"),
            P(row_axes, "gy"),
            P(row_axes, "gy"),
            P(),
        ),
        out_specs=(P(None, None, row_axes, "gy"), P(None, row_axes, "gy")),
        check_vma=False,
    )
```

```python
import functools

import jax
import jax.numpy as jnp
from jax import lax
from jax.experimental import pallas as pl
from jax.experimental.pallas import tpu as pltpu
from jax.sharding import PartitionSpec as P

SECTIONS = 5
LEVELS = 3
LOADS = 16
LANES = 128
ONE_CYCLE = 28
BOTH_CYCLES = 56

node_table = (0.35, 0.55, 0.8, 1.1, 1.5, 2.0, 2.7, 3.6)
via_conductance = 2.5
ball_conductance = 4.0
damping = 0.8
slab_partner = (0, 2, 1, 4, 3)
row_axes = ("section", "gx")


def pair_times(first, second):
    return (
        first[0] * second[0] - first[1] * second[1],
        first[0] * second[1] + first[1] * second[0],
    )


def pair_over(first, second):
    divisor = second[0] * second[0] + second[1] * second[1]
    return (
        (first[0] * second[0] + first[1] * second[1]) / divisor,
        (first[1] * second[0] - first[0] * second[1]) / divisor,
    )


def pair_minus(first, second):
    return (first[0] - second[0], first[1] - second[1])


def poly_value(coeffs, point):
    total = (0.0, 0.0)
    for c in reversed(coeffs):
        total = pair_times(total, point)
        total = (total[0] + c, total[1])
    return total


def poly_product(first, second):
    result = [0.0] * (len(first) + len(second) - 1)
    for i in range(len(first)):
        for j in range(len(second)):
            result[i + j] = result[i + j] + first[i] * second[j]
    return result


def poly_roots(coeffs):
    leading = coeffs[-1]
    scaled = [c / leading for c in coeffs]
    degree = len(coeffs) - 1
    guesses = []
    current = (1.0, 0.0)
    for k in range(degree):
        guesses.append(current)
        current = pair_times(current, (0.4, 0.9))
    for repeat_index in range(800):
        for k in range(degree):
            divisor = (1.0, 0.0)
            for j in range(degree):
                if j != k:
                    divisor = pair_times(divisor, pair_minus(guesses[k], guesses[j]))
            guesses[k] = pair_minus(guesses[k], pair_over(poly_value(scaled, guesses[k]), divisor))
    return guesses


def matrix_product(first, second):
    return [
        [
            sum((first[i][k] * second[k][j] for k in range(len(second))))
            for j in range(len(second[0]))
        ]
        for i in range(len(first))
    ]


def matrix_inverse(matrix):
    order = len(matrix)
    work = [list(matrix[i]) + [1.0 if i == j else 0.0 for j in range(order)] for i in range(order)]
    for column in range(order):
        pivot = column
        for i in range(column + 1, order):
            if abs(work[i][column]) > abs(work[pivot][column]):
                pivot = i
        work[column], work[pivot] = (work[pivot], work[column])
        factor = work[column][column]
        work[column] = [entry / factor for entry in work[column]]
        for i in range(order):
            if i != column:
                scale_row = work[i][column]
                work[i] = [work[i][j] - scale_row * work[column][j] for j in range(2 * order)]
    return [row[order:] for row in work]


def eigen_vector(matrix, value):
    order = len(matrix)
    size_inner = order - 1
    system = []
    for i in range(size_inner):
        row = []
        for j in range(order):
            entry = (matrix[i][j], 0.0)
            if i == j:
                entry = pair_minus(entry, value)
            row.append(entry)
        row[order - 1] = (-row[order - 1][0], -row[order - 1][1])
        system.append(row)
    for column in range(size_inner):
        pivot = column
        for i in range(column + 1, size_inner):
            left_size = system[i][column][0] ** 2 + system[i][column][1] ** 2
            right_size = system[pivot][column][0] ** 2 + system[pivot][column][1] ** 2
            if left_size > right_size:
                pivot = i
        system[column], system[pivot] = (system[pivot], system[column])
        for i in range(size_inner):
            if i != column:
                factor = pair_over(system[i][column], system[column][column])
                system[i] = [
                    pair_minus(system[i][j], pair_times(factor, system[column][j]))
                    for j in range(order)
                ]
    vector = [pair_over(system[i][order - 1], system[i][i]) for i in range(size_inner)]
    vector.append((1.0, 0.0))
    return vector


def radau_tables():
    section_count = 5
    generator = [1.0]
    for k in range(section_count - 1):
        generator = poly_product(generator, [0.0, 1.0])
    for k in range(section_count):
        generator = poly_product(generator, [-1.0, 1.0])
    for k in range(section_count - 1):
        generator = [j * generator[j] for j in range(1, len(generator))]
    abscissae = sorted((root[0] for root in poly_roots(generator)))
    vander = [[abscissae[i] ** j for j in range(section_count)] for i in range(section_count)]
    integrals = [
        [abscissae[i] ** (j + 1) / (j + 1) for j in range(section_count)]
        for i in range(section_count)
    ]
    butcher = matrix_product(integrals, matrix_inverse(vander))
    inverse = matrix_inverse(butcher)
    coeffs = [0.0] * (section_count + 1)
    coeffs[section_count] = 1.0
    current = [[0.0] * section_count for _ in range(section_count)]
    for k in range(1, section_count + 1):
        current = matrix_product(inverse, current)
        for i in range(section_count):
            current[i][i] = current[i][i] + coeffs[section_count - k + 1]
        applied = matrix_product(inverse, current)
        coeffs[section_count - k] = -sum((applied[i][i] for i in range(section_count))) / k
    eigen_values = poly_roots(coeffs)
    real_pick = 0
    for k in range(section_count):
        if abs(eigen_values[k][1]) < abs(eigen_values[real_pick][1]):
            real_pick = k
    upper_half = [k for k in range(section_count) if eigen_values[k][1] > 1e-09]
    upper_half = sorted(upper_half, key=lambda k: -eigen_values[k][0])
    columns = [[entry[0] for entry in eigen_vector(inverse, (eigen_values[real_pick][0], 0.0))]]
    for k in upper_half:
        vector = eigen_vector(inverse, eigen_values[k])
        columns.append([entry[0] for entry in vector])
        columns.append([entry[1] for entry in vector])
    transform = [[columns[j][i] for j in range(section_count)] for i in range(section_count)]
    inverse_transform = matrix_inverse(transform)
    blocks = matrix_product(matrix_product(inverse_transform, inverse), transform)
    diagonal = [blocks[k][k] for k in range(section_count)]
    coupling = [
        blocks[k][slab_partner[k]] if slab_partner[k] != k else 0.0 for k in range(section_count)
    ]
    return (transform, inverse_transform, diagonal, coupling)


def series(near_side, far_side):
    return 2.0 * near_side * far_side / (near_side + far_side)


def left_by(value, count):
    return pltpu.roll(value, LANES - count, axis=1)


def right_by(value, count):
    return pltpu.roll(value, count, axis=1)


def from_above(value):
    return pltpu.roll(value, value.shape[0] - 1, axis=0)


def from_below(value):
    return pltpu.roll(value, 1, axis=0)


def lane_ids(layers):
    return lax.broadcasted_iota(jnp.int32, (layers, LANES), 1)


def layer_ids(layers):
    return lax.broadcasted_iota(jnp.int32, (layers, LANES), 0)


def flux(here, ahead, behind_flux, gx, gy, gv, stride):
    along_x = gx * (ahead - here)
    along_y = gy * (left_by(here, stride) - here)
    along_z = gv * (from_above(here) - here)
    total = (
        (along_x - behind_flux)
        + (along_y - right_by(along_y, stride))
        + (along_z - from_below(along_z))
    )
    return along_x, total


def group_lanes(value, stride, low_half):
    return value + jnp.where(low_half, left_by(value, stride), right_by(value, stride))


def weights(cap, total, lam0, alpha, beta):
    real = lam0 * cap + total
    mate = beta * cap
    both = alpha * cap + total
    scale = damping / (both * both + mate * mate)
    return damping / real, both * scale, mate * scale


def correct(residual, sw0, sw, mw):
    return (
        sw0 * residual[0],
        sw * residual[1] - mw * residual[2],
        sw * residual[2] + mw * residual[1],
    )


def sweep(level, refs, scal, add=None, coarse=None):
    lam0, alpha, beta = scal
    g, x_ref, f_ref = refs[level]
    rows = g.shape[1]
    layers = g.shape[2]
    stride = 2**level
    step = min(4, rows)
    zero = jnp.zeros((layers, LANES), jnp.float32)

    def value(k, base, half, r):
        loaded = x_ref[k, base + r]
        if add is not None:
            loaded = loaded + add[k, half + r // 2]
        return loaded

    def body(b, carry):
        behind = list(carry[:3])
        xs = [[carry[3 + k]] for k in range(3)]
        base = b * step
        half = b * (step // 2)
        for k in range(3):
            for r in range(1, step + 1):
                xs[k].append(value(k, base, half, r))
        results = []
        for r in range(step):
            i = base + r
            gx, gy, gv = g[0, i], g[1, i], g[2, i]
            ground, cap = g[3, i], g[4, i]
            local = (lam0 * cap + ground, alpha * cap + ground)
            mate = beta * cap
            x0, x1, x2 = xs[0][r], xs[1][r], xs[2][r]
            pulled = []
            for k in range(3):
                behind[k], total = flux(xs[k][r], xs[k][r + 1], behind[k], gx, gy, gv, stride)
                pulled.append(total)
            residual = (
                f_ref[0, i] - local[0] * x0 + pulled[0],
                f_ref[1, i] - local[1] * x1 - mate * x2 + pulled[1],
                f_ref[2, i] - local[1] * x2 + mate * x1 + pulled[2],
            )
            if coarse is None:
                change = correct(residual, g[5, i], g[6, i], g[7, i])
                results.append([xs[k][r] + change[k] for k in range(3)])
            else:
                results.append(residual)
        if coarse is None:
            for r in range(step):
                for k in range(3):
                    x_ref[k, base + r] = results[r][k]
        else:
            g_next, x_next, f_next = refs[level + 1]
            low_half = (lane_ids(layers) // stride) % 2 == 0
            for r in range(0, step, 2):
                i = half + r // 2
                summed = [
                    group_lanes(results[r][k] + results[r + 1][k], stride, low_half)
                    for k in range(3)
                ]
                first = correct(summed, g_next[5, i], g_next[6, i], g_next[7, i])
                for k in range(3):
                    f_next[k, i] = summed[k]
                    x_next[k, i] = first[k]
        return tuple(behind) + tuple(xs[k][step] for k in range(3))

    init = (zero,) * 3 + tuple(value(k, 0, 0, 0) for k in range(3))
    lax.fori_loop(0, rows // step, body, init)


def coarsen(level, refs, scal):
    g = refs[level][0]
    g_next = refs[level + 1][0]
    layers = g.shape[2]
    stride = 2**level
    rows = g_next.shape[1]
    step = min(4, rows)

    def body(b, behind):
        low_half = (lane_ids(layers) // stride) % 2 == 0
        for r in range(step):
            i = b * step + r
            j = 2 * b * step + 2 * r
            gx = group_lanes(g[0, j + 1], stride, low_half)
            crossing = g[1, j] + g[1, j + 1]
            gy = jnp.where(low_half, left_by(crossing, stride), crossing)
            gv = group_lanes(g[2, j] + g[2, j + 1], stride, low_half)
            ground = group_lanes(g[3, j] + g[3, j + 1], stride, low_half)
            cap = group_lanes(g[4, j] + g[4, j + 1], stride, low_half)
            total = gx + behind + gy + right_by(gy, 2 * stride) + gv + from_below(gv) + ground
            found = weights(cap, total, *scal)
            for k, entry in enumerate((gx, gy, gv, ground, cap) + found):
                g_next[k, i] = entry
            behind = gx
        return behind

    lax.fori_loop(0, rows // step, body, jnp.zeros((layers, LANES), jnp.float32))


def cycle(refs, scal):
    sweep(0, refs, scal)
    sweep(0, refs, scal, coarse=True)
    sweep(1, refs, scal)
    sweep(1, refs, scal, coarse=True)
    for _ in range(3):
        sweep(2, refs, scal)
    sweep(1, refs, scal, add=refs[2][1])
    sweep(1, refs, scal)
    sweep(0, refs, scal, add=refs[1][1])
    sweep(0, refs, scal)


def kernel(
    sizes, tables, load_table, voltage, capacity, node_class, via_sites, ball_sites, load_type,
    sections, next_voltage,
    planes, edge, edge_in, send, recv, surf, g0, g1, g2, x0, x1, x2, f0, f1, f2,
    packed, landed, out_buf, out_recv,
    edge_send, edge_recv, send_sem, recv_sem, pass_send, pass_recv,
    ring_send, ring_recv, out_send, out_recv_sem, own_sem,
):
    parts, gx_count, gy_count, width, margin, columns = sizes
    transform, inverse_transform, diagonal, coupling = tables
    layers = voltage.shape[0]
    block = voltage.shape[1]
    wide = voltage.shape[2]
    tiles = wide // LANES
    regions = parts // 2
    count = 4 * block + 1
    section_here = lax.axis_index("section")
    gx_here = lax.axis_index("gx")
    gy_here = lax.axis_index("gy")
    mine = section_here * gx_count + gx_here
    system = section_here % 2
    all_regions = regions * gy_count

    def snake(place, row):
        return place + (row % 2) * (gx_count - 1 - 2 * place)

    def turned(place, column):
        return place + (column % 2) * (regions - 1 - 2 * place)

    pair = section_here // 2
    spot = turned(pair * gx_count + snake(gx_here, pair), gy_here)
    region = gy_here * regions + spot

    def owner(place, column):
        found = turned(place, column)
        row = found // gx_count
        return row * 2 + system, snake(found % gx_count, row)

    def group_device(index):
        return {"section": index // gx_count, "gx": index % gx_count}

    def region_device(index):
        column = index // regions
        owner_section, owner_gx = owner(index % regions, column)
        return {"section": owner_section, "gx": owner_gx, "gy": column}

    after = region_device((region + 1) % all_regions)
    before = region_device((region + all_regions - 1) % all_regions)
    right = {"gy": (gy_here + 1) % gy_count}
    left = {"gy": (gy_here + gy_count - 1) % gy_count}
    partner = {"section": section_here + 1 - 2 * system}

    barrier = pltpu.get_barrier_semaphore()
    friends = [group_device((mine + d) % parts) for d in range(1, parts)]
    friends += [after, before, right, left]
    for place in friends:
        pl.semaphore_signal(
            barrier, inc=1, device_id=place, device_id_type=pl.DeviceIdType.MESH
        )

    def remote(source, target, source_sem, target_sem, place):
        return pltpu.make_async_remote_copy(
            src_ref=source,
            dst_ref=target,
            send_sem=source_sem,
            recv_sem=target_sem,
            device_id=place,
            device_id_type=pl.DeviceIdType.MESH,
        )

    lanes = lane_ids(layers)
    zero = jnp.zeros((layers, LANES), jnp.float32)

    def turn_by(value, amount):
        amount = amount % LANES
        return right_by(value, amount) if amount else value

    for tile in range(tiles):
        place = pl.ds(tile * LANES, LANES)
        kind = node_class[:, :, place]
        conduct = jnp.full(kind.shape, node_table[0], jnp.float32)
        for k in range(1, len(node_table)):
            conduct = jnp.where(kind == k, jnp.float32(node_table[k]), conduct)
        via = jnp.where(via_sites[:, :, place] == 1, jnp.float32(via_conductance), 0.0)
        ball = jnp.where(ball_sites[:, place] == 1, jnp.float32(ball_conductance), 0.0)
        sites = jnp.concatenate([via, ball[None]], axis=0)
        for k, value in enumerate((voltage[:, :, place], capacity[:, :, place], conduct, sites)):
            swapped = jnp.swapaxes(value, 0, 1)
            for r in range(block):
                planes[4 * r + k, :, place] = swapped[r]
        planes[4 * block, :, place] = load_type[:, place].astype(jnp.float32)

    share = LANES // margin
    packs = edge.shape[1]
    for side, begin in ((0, LANES - margin), (1, 0)):
        place = pl.ds((tiles - 1) * LANES if side == 0 else 0, LANES)
        for q in range(packs):
            joint = zero
            for t in range(share):
                plane = q + packs * t
                if plane < count:
                    moved = turn_by(planes[plane, :, place], margin * t - begin)
                    joint = jnp.where(lanes // margin == t, moved, joint)
            edge[side, q] = joint
    pl.semaphore_wait(barrier, parts + 3)
    edges = [
        remote(edge.at[i], edge_in.at[i], edge_send.at[i], edge_recv.at[i], place)
        for i, place in ((0, right), (1, left))
    ]
    for copy in edges:
        copy.start()

    def build(k):
        start = width * k - margin
        for plane in range(count):
            q, t = plane % packs, plane // packs
            joint = None
            for tile in range(-1, tiles + 1):
                low = tile * LANES if tile >= 0 else -margin
                high = (tile + 1) * LANES if tile >= 0 else 0
                if tile == tiles:
                    high = low + margin
                if high <= start or low >= start + LANES:
                    continue
                if tile < 0:
                    moved = turn_by(edge_in[0, q], -margin - start - margin * t)
                elif tile == tiles:
                    moved = turn_by(edge_in[1, q], wide - start - margin * t)
                else:
                    moved = turn_by(planes[plane, :, pl.ds(low, LANES)], low - start)
                joint = moved if joint is None else jnp.where(lanes >= low - start, moved, joint)
            send[k, plane] = joint

    def direct(d, k):
        owner_section, owner_gx = owner(k, gy_here)
        return remote(
            send.at[k], recv.at[mine], send_sem.at[d], recv_sem.at[d],
            {"section": owner_section, "gx": owner_gx},
        )

    def handed(d, source, slot):
        return remote(source, recv.at[slot], pass_send.at[d], pass_recv.at[d], partner)

    own = pltpu.make_async_copy(send.at[spot], recv.at[mine], own_sem)

    def dispatch(k):
        d = (k - spot + regions) % regions

        @pl.when(d != 0)
        def _():
            direct(d, k).start()

        @pl.when(d == 0)
        def _():
            own.start()
            handed(0, send.at[k], mine).start()

    inner = [k for k in range(regions) if margin <= width * k <= wide - LANES + margin]
    outer = [k for k in range(regions) if k not in inner]
    for k in inner:
        build(k)
    for k in inner:
        dispatch(k)
    for copy in edges:
        copy.wait()
    for k in outer:
        build(k)
    for k in outer:
        dispatch(k)

    def pick(table):
        return [
            jnp.where(system == 0, jnp.float32(table[a]), jnp.float32(table[b]))
            for a, b in ((0, 0), (1, 3), (2, 4))
        ]

    shifts = pick(diagonal)
    lam0, alpha, beta = shifts[0], shifts[1], pick(coupling)[1]
    shares = pick([sum(row) for row in inverse_transform])
    mixing = [pick([row[j] for row in inverse_transform]) for j in range(SECTIONS)]
    scal = (lam0, alpha, beta)
    for x_ref in (x0, x1, x2):
        for k in range(3):
            x_ref[k, x_ref.shape[1] - 1] = zero
    passes = [handed(0, send.at[spot], mine)]
    for d in range(1, regions):
        direct(d, (spot + d) % regions).wait()
        owner_section, owner_gx = owner((spot - d + regions) % regions, gy_here)
        slot = owner_section * gx_count + owner_gx
        copy = handed(d, recv.at[slot], slot)
        copy.start()
        passes.append(copy)
    own.wait()
    for copy in passes:
        copy.wait()

    def loads(b, carry):
        kind = recv[b, 4 * block]
        currents = [zero] * SECTIONS
        for t in range(LOADS):
            here = kind == float(t)
            for j in range(SECTIONS):
                currents[j] = jnp.where(here, load_table[t, j], currents[j])
        for k in range(3):
            surf[k, b] = sum(mixing[j][k] * currents[j] for j in range(SECTIONS))
        return carry

    lax.fori_loop(0, parts, loads, 0)

    rows = parts * block
    level_of = layer_ids(layers)
    column = region * width - margin + lanes
    inside = (column >= 0) & (column < columns)
    joined = inside & (column < columns - 1) & (lanes < LANES - 1)

    def fine(b, carry):
        behind_gx, behind_flux = carry
        following = jnp.minimum(b + 1, parts - 1)
        for r in range(block):
            i = b * block + r
            volt, cap = recv[b, 4 * r], recv[b, 4 * r + 1]
            conduct = jnp.where(inside, recv[b, 4 * r + 2], 1.0)
            sites = recv[b, 4 * r + 3]
            if r + 1 < block:
                volt_ahead, conduct_ahead = recv[b, 4 * r + 4], recv[b, 4 * r + 6]
            else:
                volt_ahead, conduct_ahead = recv[following, 0], recv[following, 2]
            conduct_ahead = jnp.where(inside, conduct_ahead, 1.0)
            gx = series(conduct, conduct_ahead)
            if r + 1 == block:
                gx = gx * (b < parts - 1).astype(jnp.float32)
            gy = jnp.where(joined, series(conduct, left_by(conduct, 1)), 0.0)
            gv = jnp.where(level_of < layers - 1, sites, 0.0)
            ground = jnp.where(level_of == 0, from_below(sites), 0.0)
            total = gx + behind_gx + gy + right_by(gy, 1) + gv + from_below(gv) + ground
            found = weights(cap, total, *scal)
            behind_flux, pulled = flux(volt, volt_ahead, behind_flux, gx, gy, gv, 1)
            leak = ground * volt - pulled
            for k, entry in enumerate((gx, gy, gv, ground, cap) + found):
                g0[k, i] = entry
            source = [
                jnp.where(
                    level_of == layers - 1,
                    jnp.broadcast_to(surf[k, b, r : r + 1, :], (layers, LANES)),
                    0.0,
                )
                - shares[k] * leak
                for k in range(3)
            ]
            first = correct(source, *found)
            for k in range(3):
                f0[k, i] = source[k]
                x0[k, i] = first[k]
            behind_gx = gx
        return behind_gx, behind_flux

    lax.fori_loop(0, parts, fine, (zero, zero))
    refs = ((g0, x0, f0), (g1, x1, f1), (g2, x2, f2))
    coarsen(0, refs, scal)
    coarsen(1, refs, scal)
    cycle(refs, scal)

    if margin < BOTH_CYCLES:
        share = LANES // margin
        groups = rows // share

        def pack(q, carry):
            for side, begin in ((0, width), (1, margin)):
                for k in range(3):
                    joint = zero
                    for t in range(share):
                        turn = (margin * t - begin) % LANES
                        moved = x0[k, q + groups * t]
                        if turn:
                            moved = right_by(moved, turn)
                        joint = jnp.where(lanes // margin == t, moved, joint)
                    packed[side, k, q] = joint
            return carry

        lax.fori_loop(0, groups, pack, 0)
        ring = []
        for side, place in ((0, after), (1, before)):
            copy = pltpu.make_async_remote_copy(
                src_ref=packed.at[side],
                dst_ref=landed.at[side],
                send_sem=ring_send.at[side],
                recv_sem=ring_recv.at[side],
                device_id=place,
                device_id_type=pl.DeviceIdType.MESH,
            )
            copy.start()
            ring.append(copy)
        for copy in ring:
            copy.wait()

        def unpack(q, carry):
            for k in range(3):
                low = landed[0, k, q]
                high = landed[1, k, q]
                for t in range(share):
                    turn_low = (-margin * t) % LANES
                    turn_high = (margin + width - margin * t) % LANES
                    a = right_by(low, turn_low) if turn_low else low
                    c = right_by(high, turn_high) if turn_high else high
                    x = x0[k, q + groups * t]
                    x = jnp.where(lanes < margin, a, jnp.where(lanes < margin + width, x, c))
                    x0[k, q + groups * t] = x
            return carry

        lax.fori_loop(0, groups, unpack, 0)

    sweep(0, refs, scal)
    cycle(refs, scal)

    share = LANES // width
    groups = block // share
    half = max(groups // 2, 1)
    halves = groups // half
    slot_out = spot * 2 + system
    copies = []
    for d in range(parts):
        peer = (mine + d) % parts
        for index in range(half + 2 * groups):
            k = 0 if index < half else 1 + (index - half) // groups
            if k == 0:
                q = index + (system * half if halves > 1 else 0)
            else:
                q = (index - half) % groups
            joint = zero
            for t in range(share):
                moved = turn_by(x0[k, peer * block + q + groups * t], width * t - margin)
                joint = jnp.where(lanes // width == t, moved, joint)
            out_buf[d, index] = joint
        if d == 0:
            own = pltpu.make_async_copy(out_buf.at[0], out_recv.at[slot_out], own_sem)
            own.start()
            continue
        copy = pltpu.make_async_remote_copy(
            src_ref=out_buf.at[d],
            dst_ref=out_recv.at[slot_out],
            send_sem=out_send.at[d],
            recv_sem=out_recv_sem.at[d],
            device_id=group_device(peer),
            device_id_type=pl.DeviceIdType.MESH,
        )
        copy.start()
        copies.append(copy)
    own.wait()
    for copy in copies:
        copy.wait()

    for tile in range(regions // share):
        mixed = [[None] * block for _ in range(SECTIONS)]
        for q in range(groups):
            fields = []
            for n in range(share):
                first = 2 * (tile * share + n)
                fields.append(
                    [out_recv[first + q // half, q % half]]
                    + [out_recv[first, half + k * groups + q] for k in (0, 1)]
                    + [out_recv[first + 1, half + k * groups + q] for k in (0, 1)]
                )
            for s in range(SECTIONS):
                sums = [
                    sum(transform[s][k] * fields[n][k] for k in range(SECTIONS))
                    for n in range(share)
                ]
                for t in range(share):
                    joint = zero
                    for n in range(share):
                        turn = (width * (n - t)) % LANES
                        moved = right_by(sums[n], turn) if turn else sums[n]
                        joint = jnp.where(lanes // width == n, moved, joint)
                    mixed[s][q + groups * t] = joint
        place = pl.ds(tile * LANES, LANES)
        for s in range(SECTIONS):
            turned = jnp.swapaxes(jnp.stack(mixed[s]), 0, 1)
            sections[s, :, :, place] = turned
            if s == SECTIONS - 1:
                next_voltage[:, :, place] = voltage[:, :, place] + turned


def local(voltage, capacity, node_class, via_sites, ball_sites, load_type, load_table):
    layers, block, wide = voltage.shape
    gx_count = lax.axis_size("gx")
    gy_count = lax.axis_size("gy")
    parts = lax.axis_size("section") * gx_count
    regions = parts // 2
    width = wide // regions
    margin = (LANES - width) // 2
    sizes = (parts, gx_count, gy_count, width, margin, wide * gy_count)
    rows = parts * block
    count = 4 * block + 1
    packs = -(-count // (LANES // margin))

    def vmem(*shape):
        return pltpu.VMEM(shape, jnp.float32)

    def levels(count, extra):
        return [vmem(count, rows // 2**m + extra, layers, LANES) for m in range(LEVELS)]

    mid = rows * margin // LANES if margin < BOTH_CYCLES else 1
    groups = block * width // LANES
    back = max(groups // 2, 1) + 2 * groups
    return pl.pallas_call(
        functools.partial(kernel, sizes, radau_tables()),
        out_shape=(
            jax.ShapeDtypeStruct((SECTIONS, layers, block, wide), jnp.float32),
            jax.ShapeDtypeStruct((layers, block, wide), jnp.float32),
        ),
        in_specs=[
            pl.BlockSpec(memory_space=pltpu.SMEM),
            *[pl.BlockSpec(memory_space=pltpu.VMEM)] * 6,
        ],
        out_specs=(
            pl.BlockSpec(memory_space=pltpu.VMEM),
            pl.BlockSpec(memory_space=pltpu.VMEM),
        ),
        scratch_shapes=[
            vmem(count, layers, wide),
            vmem(2, packs, layers, LANES),
            vmem(2, packs, layers, LANES),
            vmem(regions, count, layers, LANES),
            vmem(parts, count, layers, LANES),
            vmem(3, parts, block, LANES),
            *levels(8, 0),
            *levels(3, 1),
            *levels(3, 0),
            vmem(2, 3, mid, layers, LANES),
            vmem(2, 3, mid, layers, LANES),
            vmem(parts, back, layers, LANES),
            vmem(parts, back, layers, LANES),
            pltpu.SemaphoreType.DMA((2,)),
            pltpu.SemaphoreType.DMA((2,)),
            pltpu.SemaphoreType.DMA((regions,)),
            pltpu.SemaphoreType.DMA((regions,)),
            pltpu.SemaphoreType.DMA((regions,)),
            pltpu.SemaphoreType.DMA((regions,)),
            pltpu.SemaphoreType.DMA((2,)),
            pltpu.SemaphoreType.DMA((2,)),
            pltpu.SemaphoreType.DMA((parts,)),
            pltpu.SemaphoreType.DMA((parts,)),
            pltpu.SemaphoreType.DMA,
        ],
        compiler_params=pltpu.CompilerParams(
            collective_id=0, has_side_effects=True, vmem_limit_bytes=60 * 1024 * 1024
        ),
    )(load_table, voltage, capacity, node_class, via_sites, ball_sites, load_type)


def solution(mesh):
    return jax.shard_map(
        local,
        mesh=mesh,
        in_specs=(
            P(None, row_axes, "gy"),
            P(None, row_axes, "gy"),
            P(None, row_axes, "gy"),
            P(None, row_axes, "gy"),
            P(row_axes, "gy"),
            P(row_axes, "gy"),
            P(),
        ),
        out_specs=(P(None, None, row_axes, "gy"), P(None, row_axes, "gy")),
        check_vma=False,
    )
```

```python
import functools

import jax
import jax.numpy as jnp
from jax import lax
from jax.experimental import pallas as pl
from jax.experimental.pallas import tpu as pltpu
from jax.sharding import PartitionSpec as P

SECTIONS = 5
LEVELS = 3
LOADS = 16
LANES = 128
ONE_CYCLE = 28
BOTH_CYCLES = 56

node_table = (0.35, 0.55, 0.8, 1.1, 1.5, 2.0, 2.7, 3.6)
via_conductance = 2.5
ball_conductance = 4.0
damping = 0.8
slab_partner = (0, 2, 1, 4, 3)
row_axes = ("section", "gx")


def pair_times(first, second):
    return (
        first[0] * second[0] - first[1] * second[1],
        first[0] * second[1] + first[1] * second[0],
    )


def pair_over(first, second):
    divisor = second[0] * second[0] + second[1] * second[1]
    return (
        (first[0] * second[0] + first[1] * second[1]) / divisor,
        (first[1] * second[0] - first[0] * second[1]) / divisor,
    )


def pair_minus(first, second):
    return (first[0] - second[0], first[1] - second[1])


def poly_value(coeffs, point):
    total = (0.0, 0.0)
    for c in reversed(coeffs):
        total = pair_times(total, point)
        total = (total[0] + c, total[1])
    return total


def poly_product(first, second):
    result = [0.0] * (len(first) + len(second) - 1)
    for i in range(len(first)):
        for j in range(len(second)):
            result[i + j] = result[i + j] + first[i] * second[j]
    return result


def poly_roots(coeffs):
    leading = coeffs[-1]
    scaled = [c / leading for c in coeffs]
    degree = len(coeffs) - 1
    guesses = []
    current = (1.0, 0.0)
    for k in range(degree):
        guesses.append(current)
        current = pair_times(current, (0.4, 0.9))
    for repeat_index in range(800):
        for k in range(degree):
            divisor = (1.0, 0.0)
            for j in range(degree):
                if j != k:
                    divisor = pair_times(divisor, pair_minus(guesses[k], guesses[j]))
            guesses[k] = pair_minus(guesses[k], pair_over(poly_value(scaled, guesses[k]), divisor))
    return guesses


def matrix_product(first, second):
    return [
        [
            sum((first[i][k] * second[k][j] for k in range(len(second))))
            for j in range(len(second[0]))
        ]
        for i in range(len(first))
    ]


def matrix_inverse(matrix):
    order = len(matrix)
    work = [list(matrix[i]) + [1.0 if i == j else 0.0 for j in range(order)] for i in range(order)]
    for column in range(order):
        pivot = column
        for i in range(column + 1, order):
            if abs(work[i][column]) > abs(work[pivot][column]):
                pivot = i
        work[column], work[pivot] = (work[pivot], work[column])
        factor = work[column][column]
        work[column] = [entry / factor for entry in work[column]]
        for i in range(order):
            if i != column:
                scale_row = work[i][column]
                work[i] = [work[i][j] - scale_row * work[column][j] for j in range(2 * order)]
    return [row[order:] for row in work]


def eigen_vector(matrix, value):
    order = len(matrix)
    size_inner = order - 1
    system = []
    for i in range(size_inner):
        row = []
        for j in range(order):
            entry = (matrix[i][j], 0.0)
            if i == j:
                entry = pair_minus(entry, value)
            row.append(entry)
        row[order - 1] = (-row[order - 1][0], -row[order - 1][1])
        system.append(row)
    for column in range(size_inner):
        pivot = column
        for i in range(column + 1, size_inner):
            left_size = system[i][column][0] ** 2 + system[i][column][1] ** 2
            right_size = system[pivot][column][0] ** 2 + system[pivot][column][1] ** 2
            if left_size > right_size:
                pivot = i
        system[column], system[pivot] = (system[pivot], system[column])
        for i in range(size_inner):
            if i != column:
                factor = pair_over(system[i][column], system[column][column])
                system[i] = [
                    pair_minus(system[i][j], pair_times(factor, system[column][j]))
                    for j in range(order)
                ]
    vector = [pair_over(system[i][order - 1], system[i][i]) for i in range(size_inner)]
    vector.append((1.0, 0.0))
    return vector


def radau_tables():
    section_count = 5
    generator = [1.0]
    for k in range(section_count - 1):
        generator = poly_product(generator, [0.0, 1.0])
    for k in range(section_count):
        generator = poly_product(generator, [-1.0, 1.0])
    for k in range(section_count - 1):
        generator = [j * generator[j] for j in range(1, len(generator))]
    abscissae = sorted((root[0] for root in poly_roots(generator)))
    vander = [[abscissae[i] ** j for j in range(section_count)] for i in range(section_count)]
    integrals = [
        [abscissae[i] ** (j + 1) / (j + 1) for j in range(section_count)]
        for i in range(section_count)
    ]
    butcher = matrix_product(integrals, matrix_inverse(vander))
    inverse = matrix_inverse(butcher)
    coeffs = [0.0] * (section_count + 1)
    coeffs[section_count] = 1.0
    current = [[0.0] * section_count for _ in range(section_count)]
    for k in range(1, section_count + 1):
        current = matrix_product(inverse, current)
        for i in range(section_count):
            current[i][i] = current[i][i] + coeffs[section_count - k + 1]
        applied = matrix_product(inverse, current)
        coeffs[section_count - k] = -sum((applied[i][i] for i in range(section_count))) / k
    eigen_values = poly_roots(coeffs)
    real_pick = 0
    for k in range(section_count):
        if abs(eigen_values[k][1]) < abs(eigen_values[real_pick][1]):
            real_pick = k
    upper_half = [k for k in range(section_count) if eigen_values[k][1] > 1e-09]
    upper_half = sorted(upper_half, key=lambda k: -eigen_values[k][0])
    columns = [[entry[0] for entry in eigen_vector(inverse, (eigen_values[real_pick][0], 0.0))]]
    for k in upper_half:
        vector = eigen_vector(inverse, eigen_values[k])
        columns.append([entry[0] for entry in vector])
        columns.append([entry[1] for entry in vector])
    transform = [[columns[j][i] for j in range(section_count)] for i in range(section_count)]
    inverse_transform = matrix_inverse(transform)
    blocks = matrix_product(matrix_product(inverse_transform, inverse), transform)
    diagonal = [blocks[k][k] for k in range(section_count)]
    coupling = [
        blocks[k][slab_partner[k]] if slab_partner[k] != k else 0.0 for k in range(section_count)
    ]
    return (transform, inverse_transform, diagonal, coupling)


def series(near_side, far_side):
    return 2.0 * near_side * far_side / (near_side + far_side)


def left_by(value, count):
    return pltpu.roll(value, LANES - count, axis=1)


def right_by(value, count):
    return pltpu.roll(value, count, axis=1)


def from_above(value):
    return pltpu.roll(value, value.shape[0] - 1, axis=0)


def from_below(value):
    return pltpu.roll(value, 1, axis=0)


def lane_ids(layers):
    return lax.broadcasted_iota(jnp.int32, (layers, LANES), 1)


def layer_ids(layers):
    return lax.broadcasted_iota(jnp.int32, (layers, LANES), 0)


def flux(here, ahead, behind_flux, gx, gy, gv, stride, gy_low=None, gv_low=None):
    if gy_low is None:
        gy_low, gv_low = right_by(gy, stride), from_below(gv)
    along_x = gx * (ahead - here)
    total = (
        (along_x - behind_flux)
        + (gy * (left_by(here, stride) - here) + gy_low * (right_by(here, stride) - here))
        + (gv * (from_above(here) - here) + gv_low * (from_below(here) - here))
    )
    return along_x, total


def group_lanes(value, stride, low_half):
    return value + jnp.where(low_half, left_by(value, stride), right_by(value, stride))


def weights(cap, total, lam0, alpha, beta):
    real = lam0 * cap + total
    mate = beta * cap
    both = alpha * cap + total
    scale = damping / (both * both + mate * mate)
    return damping / real, both * scale, mate * scale


def correct(residual, sw0, sw, mw):
    return (
        sw0 * residual[0],
        sw * residual[1] - mw * residual[2],
        sw * residual[2] + mw * residual[1],
    )


def sweep(level, refs, scal, add=None, coarse=None):
    lam0, alpha, beta = scal
    g, x_ref, f_ref = refs[level]
    rows = g.shape[1]
    layers = g.shape[2]
    stride = 2**level
    step = min(16, rows)
    zero = jnp.zeros((layers, LANES), jnp.float32)

    def value(k, base, half, r):
        loaded = x_ref[k, base + r]
        if add is not None:
            loaded = loaded + add[k, half + r // 2]
        return loaded

    def body(b, carry):
        behind = list(carry[:3])
        xs = [[carry[3 + k]] for k in range(3)]
        base = b * step
        half = b * (step // 2)
        for k in range(3):
            for r in range(1, step + 1):
                xs[k].append(value(k, base, half, r))
        results = []
        for r in range(step):
            i = base + r
            gx, gy, gv = g[0, i], g[1, i], g[2, i]
            ground, cap = g[3, i], g[4, i]
            gy_low, gv_low = g[8, i], g[9, i]
            local = (lam0 * cap + ground, alpha * cap + ground)
            mate = beta * cap
            x0, x1, x2 = xs[0][r], xs[1][r], xs[2][r]
            pulled = []
            for k in range(3):
                behind[k], total = flux(xs[k][r], xs[k][r + 1], behind[k], gx, gy, gv, stride, gy_low, gv_low)
                pulled.append(total)
            residual = (
                f_ref[0, i] - local[0] * x0 + pulled[0],
                f_ref[1, i] - local[1] * x1 - mate * x2 + pulled[1],
                f_ref[2, i] - local[1] * x2 + mate * x1 + pulled[2],
            )
            if coarse is None:
                change = correct(residual, g[5, i], g[6, i], g[7, i])
                results.append([xs[k][r] + change[k] for k in range(3)])
            else:
                results.append(residual)
        if coarse is None:
            for r in range(step):
                for k in range(3):
                    x_ref[k, base + r] = results[r][k]
        else:
            g_next, x_next, f_next = refs[level + 1]
            low_half = (lane_ids(layers) // stride) % 2 == 0
            for r in range(0, step, 2):
                i = half + r // 2
                summed = [
                    group_lanes(results[r][k] + results[r + 1][k], stride, low_half)
                    for k in range(3)
                ]
                first = correct(summed, g_next[5, i], g_next[6, i], g_next[7, i])
                for k in range(3):
                    f_next[k, i] = summed[k]
                    x_next[k, i] = first[k]
        return tuple(behind) + tuple(xs[k][step] for k in range(3))

    init = (zero,) * 3 + tuple(value(k, 0, 0, 0) for k in range(3))
    lax.fori_loop(0, rows // step, body, init)


def coarsen(level, refs, scal):
    g = refs[level][0]
    g_next = refs[level + 1][0]
    layers = g.shape[2]
    stride = 2**level
    rows = g_next.shape[1]
    step = min(4, rows)

    def body(b, behind):
        low_half = (lane_ids(layers) // stride) % 2 == 0
        for r in range(step):
            i = b * step + r
            j = 2 * b * step + 2 * r
            gx = group_lanes(g[0, j + 1], stride, low_half)
            crossing = g[1, j] + g[1, j + 1]
            gy = jnp.where(low_half, left_by(crossing, stride), crossing)
            gv = group_lanes(g[2, j] + g[2, j + 1], stride, low_half)
            ground = group_lanes(g[3, j] + g[3, j + 1], stride, low_half)
            cap = group_lanes(g[4, j] + g[4, j + 1], stride, low_half)
            total = gx + behind + gy + right_by(gy, 2 * stride) + gv + from_below(gv) + ground
            found = weights(cap, total, *scal)
            lows = (right_by(gy, 2 * stride), from_below(gv))
            for k, entry in enumerate((gx, gy, gv, ground, cap) + found + lows):
                g_next[k, i] = entry
            behind = gx
        return behind

    lax.fori_loop(0, rows // step, body, jnp.zeros((layers, LANES), jnp.float32))


def cycle(refs, scal):
    sweep(0, refs, scal)
    sweep(0, refs, scal, coarse=True)
    sweep(1, refs, scal)
    sweep(1, refs, scal, coarse=True)
    for _ in range(3):
        sweep(2, refs, scal)
    sweep(1, refs, scal, add=refs[2][1])
    sweep(1, refs, scal)
    sweep(0, refs, scal, add=refs[1][1])
    sweep(0, refs, scal)


def kernel(
    sizes, tables, load_table, voltage, capacity, node_class, via_sites, ball_sites, load_type,
    sections, next_voltage,
    planes, edge, edge_in, send, recv, surf, g0, g1, g2, x0, x1, x2, f0, f1, f2,
    packed, landed, out_buf, out_recv,
    edge_send, edge_recv, send_sem, recv_sem, pass_send, pass_recv,
    ring_send, ring_recv, out_send, out_recv_sem, own_sem,
):
    parts, gx_count, gy_count, width, margin, columns = sizes
    transform, inverse_transform, diagonal, coupling = tables
    layers = voltage.shape[0]
    block = voltage.shape[1]
    wide = voltage.shape[2]
    tiles = wide // LANES
    regions = parts // 2
    count = 4 * block + 1
    section_here = lax.axis_index("section")
    gx_here = lax.axis_index("gx")
    gy_here = lax.axis_index("gy")
    mine = section_here * gx_count + gx_here
    system = section_here % 2
    all_regions = regions * gy_count

    def snake(place, row):
        return place + (row % 2) * (gx_count - 1 - 2 * place)

    def turned(place, column):
        return place + (column % 2) * (regions - 1 - 2 * place)

    pair = section_here // 2
    spot = turned(pair * gx_count + snake(gx_here, pair), gy_here)
    region = gy_here * regions + spot

    def owner(place, column):
        found = turned(place, column)
        row = found // gx_count
        return row * 2 + system, snake(found % gx_count, row)

    def group_device(index):
        return {"section": index // gx_count, "gx": index % gx_count}

    def region_device(index):
        column = index // regions
        owner_section, owner_gx = owner(index % regions, column)
        return {"section": owner_section, "gx": owner_gx, "gy": column}

    after = region_device((region + 1) % all_regions)
    before = region_device((region + all_regions - 1) % all_regions)
    right = {"gy": (gy_here + 1) % gy_count}
    left = {"gy": (gy_here + gy_count - 1) % gy_count}
    partner = {"section": section_here + 1 - 2 * system}

    barrier = pltpu.get_barrier_semaphore()
    friends = [group_device((mine + d) % parts) for d in range(1, parts)]
    friends += [after, before, right, left]
    for place in friends:
        pl.semaphore_signal(
            barrier, inc=1, device_id=place, device_id_type=pl.DeviceIdType.MESH
        )

    def remote(source, target, source_sem, target_sem, place):
        return pltpu.make_async_remote_copy(
            src_ref=source,
            dst_ref=target,
            send_sem=source_sem,
            recv_sem=target_sem,
            device_id=place,
            device_id_type=pl.DeviceIdType.MESH,
        )

    lanes = lane_ids(layers)
    zero = jnp.zeros((layers, LANES), jnp.float32)

    def turn_by(value, amount):
        amount = amount % LANES
        return right_by(value, amount) if amount else value

    for tile in range(tiles):
        place = pl.ds(tile * LANES, LANES)
        kind = node_class[:, :, place]
        conduct = jnp.full(kind.shape, node_table[0], jnp.float32)
        for k in range(1, len(node_table)):
            conduct = jnp.where(kind == k, jnp.float32(node_table[k]), conduct)
        via = jnp.where(via_sites[:, :, place] == 1, jnp.float32(via_conductance), 0.0)
        ball = jnp.where(ball_sites[:, place] == 1, jnp.float32(ball_conductance), 0.0)
        sites = jnp.concatenate([via, ball[None]], axis=0)
        for k, value in enumerate((voltage[:, :, place], capacity[:, :, place], conduct, sites)):
            swapped = jnp.swapaxes(value, 0, 1)
            for r in range(block):
                planes[4 * r + k, :, place] = swapped[r]
        planes[4 * block, :, place] = load_type[:, place].astype(jnp.float32)

    share = LANES // margin
    packs = edge.shape[1]
    for side, begin in ((0, LANES - margin), (1, 0)):
        place = pl.ds((tiles - 1) * LANES if side == 0 else 0, LANES)
        for q in range(packs):
            joint = zero
            for t in range(share):
                plane = q + packs * t
                if plane < count:
                    moved = turn_by(planes[plane, :, place], margin * t - begin)
                    joint = jnp.where(lanes // margin == t, moved, joint)
            edge[side, q] = joint
    pl.semaphore_wait(barrier, parts + 3)
    edges = [
        remote(edge.at[i], edge_in.at[i], edge_send.at[i], edge_recv.at[i], place)
        for i, place in ((0, right), (1, left))
    ]
    for copy in edges:
        copy.start()

    def build(k):
        start = width * k - margin
        for plane in range(count):
            q, t = plane % packs, plane // packs
            joint = None
            for tile in range(-1, tiles + 1):
                low = tile * LANES if tile >= 0 else -margin
                high = (tile + 1) * LANES if tile >= 0 else 0
                if tile == tiles:
                    high = low + margin
                if high <= start or low >= start + LANES:
                    continue
                if tile < 0:
                    moved = turn_by(edge_in[0, q], -margin - start - margin * t)
                elif tile == tiles:
                    moved = turn_by(edge_in[1, q], wide - start - margin * t)
                else:
                    moved = turn_by(planes[plane, :, pl.ds(low, LANES)], low - start)
                joint = moved if joint is None else jnp.where(lanes >= low - start, moved, joint)
            send[k, plane] = joint

    def direct(d, k):
        owner_section, owner_gx = owner(k, gy_here)
        return remote(
            send.at[k], recv.at[mine], send_sem.at[d], recv_sem.at[d],
            {"section": owner_section, "gx": owner_gx},
        )

    def handed(d, source, slot):
        return remote(source, recv.at[slot], pass_send.at[d], pass_recv.at[d], partner)

    own = pltpu.make_async_copy(send.at[spot], recv.at[mine], own_sem)

    def dispatch(k):
        d = (k - spot + regions) % regions

        @pl.when(d != 0)
        def _():
            direct(d, k).start()

        @pl.when(d == 0)
        def _():
            own.start()
            handed(0, send.at[k], mine).start()

    inner = [k for k in range(regions) if margin <= width * k <= wide - LANES + margin]
    outer = [k for k in range(regions) if k not in inner]
    for k in inner:
        build(k)
    for k in inner:
        dispatch(k)
    for copy in edges:
        copy.wait()
    for k in outer:
        build(k)
    for k in outer:
        dispatch(k)

    def pick(table):
        return [
            jnp.where(system == 0, jnp.float32(table[a]), jnp.float32(table[b]))
            for a, b in ((0, 0), (1, 3), (2, 4))
        ]

    shifts = pick(diagonal)
    lam0, alpha, beta = shifts[0], shifts[1], pick(coupling)[1]
    shares = pick([sum(row) for row in inverse_transform])
    mixing = [pick([row[j] for row in inverse_transform]) for j in range(SECTIONS)]
    scal = (lam0, alpha, beta)
    for x_ref in (x0, x1, x2):
        for k in range(3):
            x_ref[k, x_ref.shape[1] - 1] = zero
    passes = [handed(0, send.at[spot], mine)]
    for d in range(1, regions):
        direct(d, (spot + d) % regions).wait()
        owner_section, owner_gx = owner((spot - d + regions) % regions, gy_here)
        slot = owner_section * gx_count + owner_gx
        copy = handed(d, recv.at[slot], slot)
        copy.start()
        passes.append(copy)
    own.wait()
    for copy in passes:
        copy.wait()

    def loads(b, carry):
        kind = recv[b, 4 * block]
        currents = [zero] * SECTIONS
        for t in range(LOADS):
            here = kind == float(t)
            for j in range(SECTIONS):
                currents[j] = jnp.where(here, load_table[t, j], currents[j])
        for k in range(3):
            surf[k, b] = sum(mixing[j][k] * currents[j] for j in range(SECTIONS))
        return carry

    lax.fori_loop(0, parts, loads, 0)

    rows = parts * block
    level_of = layer_ids(layers)
    column = region * width - margin + lanes
    inside = (column >= 0) & (column < columns)
    joined = inside & (column < columns - 1) & (lanes < LANES - 1)

    def fine(b, carry):
        behind_gx, behind_flux = carry
        following = jnp.minimum(b + 1, parts - 1)
        for r in range(block):
            i = b * block + r
            volt, cap = recv[b, 4 * r], recv[b, 4 * r + 1]
            conduct = jnp.where(inside, recv[b, 4 * r + 2], 1.0)
            sites = recv[b, 4 * r + 3]
            if r + 1 < block:
                volt_ahead, conduct_ahead = recv[b, 4 * r + 4], recv[b, 4 * r + 6]
            else:
                volt_ahead, conduct_ahead = recv[following, 0], recv[following, 2]
            conduct_ahead = jnp.where(inside, conduct_ahead, 1.0)
            gx = series(conduct, conduct_ahead)
            if r + 1 == block:
                gx = gx * (b < parts - 1).astype(jnp.float32)
            gy = jnp.where(joined, series(conduct, left_by(conduct, 1)), 0.0)
            gv = jnp.where(level_of < layers - 1, sites, 0.0)
            ground = jnp.where(level_of == 0, from_below(sites), 0.0)
            total = gx + behind_gx + gy + right_by(gy, 1) + gv + from_below(gv) + ground
            found = weights(cap, total, *scal)
            behind_flux, pulled = flux(volt, volt_ahead, behind_flux, gx, gy, gv, 1)
            leak = ground * volt - pulled
            lows = (right_by(gy, 1), from_below(gv))
            for k, entry in enumerate((gx, gy, gv, ground, cap) + found + lows):
                g0[k, i] = entry
            source = [
                jnp.where(
                    level_of == layers - 1,
                    jnp.broadcast_to(surf[k, b, r : r + 1, :], (layers, LANES)),
                    0.0,
                )
                - shares[k] * leak
                for k in range(3)
            ]
            first = correct(source, *found)
            for k in range(3):
                f0[k, i] = source[k]
                x0[k, i] = first[k]
            behind_gx = gx
        return behind_gx, behind_flux

    lax.fori_loop(0, parts, fine, (zero, zero))
    refs = ((g0, x0, f0), (g1, x1, f1), (g2, x2, f2))
    coarsen(0, refs, scal)
    coarsen(1, refs, scal)
    cycle(refs, scal)

    if margin < BOTH_CYCLES:
        share = LANES // margin
        groups = rows // share

        def pack(q, carry):
            for side, begin in ((0, width), (1, margin)):
                for k in range(3):
                    joint = zero
                    for t in range(share):
                        turn = (margin * t - begin) % LANES
                        moved = x0[k, q + groups * t]
                        if turn:
                            moved = right_by(moved, turn)
                        joint = jnp.where(lanes // margin == t, moved, joint)
                    packed[side, k, q] = joint
            return carry

        lax.fori_loop(0, groups, pack, 0)
        ring = []
        for side, place in ((0, after), (1, before)):
            copy = pltpu.make_async_remote_copy(
                src_ref=packed.at[side],
                dst_ref=landed.at[side],
                send_sem=ring_send.at[side],
                recv_sem=ring_recv.at[side],
                device_id=place,
                device_id_type=pl.DeviceIdType.MESH,
            )
            copy.start()
            ring.append(copy)
        for copy in ring:
            copy.wait()

        def unpack(q, carry):
            for k in range(3):
                low = landed[0, k, q]
                high = landed[1, k, q]
                for t in range(share):
                    turn_low = (-margin * t) % LANES
                    turn_high = (margin + width - margin * t) % LANES
                    a = right_by(low, turn_low) if turn_low else low
                    c = right_by(high, turn_high) if turn_high else high
                    x = x0[k, q + groups * t]
                    x = jnp.where(lanes < margin, a, jnp.where(lanes < margin + width, x, c))
                    x0[k, q + groups * t] = x
            return carry

        lax.fori_loop(0, groups, unpack, 0)

    sweep(0, refs, scal)
    cycle(refs, scal)

    share = LANES // width
    groups = block // share
    half = max(groups // 2, 1)
    halves = groups // half
    slot_out = spot * 2 + system
    copies = []
    for d in range(parts):
        peer = (mine + d) % parts
        for index in range(half + 2 * groups):
            k = 0 if index < half else 1 + (index - half) // groups
            if k == 0:
                q = index + (system * half if halves > 1 else 0)
            else:
                q = (index - half) % groups
            joint = zero
            for t in range(share):
                moved = turn_by(x0[k, peer * block + q + groups * t], width * t - margin)
                joint = jnp.where(lanes // width == t, moved, joint)
            out_buf[d, index] = joint
        if d == 0:
            own = pltpu.make_async_copy(out_buf.at[0], out_recv.at[slot_out], own_sem)
            own.start()
            continue
        copy = pltpu.make_async_remote_copy(
            src_ref=out_buf.at[d],
            dst_ref=out_recv.at[slot_out],
            send_sem=out_send.at[d],
            recv_sem=out_recv_sem.at[d],
            device_id=group_device(peer),
            device_id_type=pl.DeviceIdType.MESH,
        )
        copy.start()
        copies.append(copy)
    own.wait()
    for copy in copies:
        copy.wait()

    for tile in range(regions // share):
        mixed = [[None] * block for _ in range(SECTIONS)]
        for q in range(groups):
            fields = []
            for n in range(share):
                first = 2 * (tile * share + n)
                fields.append(
                    [out_recv[first + q // half, q % half]]
                    + [out_recv[first, half + k * groups + q] for k in (0, 1)]
                    + [out_recv[first + 1, half + k * groups + q] for k in (0, 1)]
                )
            for s in range(SECTIONS):
                sums = [
                    sum(transform[s][k] * fields[n][k] for k in range(SECTIONS))
                    for n in range(share)
                ]
                for t in range(share):
                    joint = zero
                    for n in range(share):
                        turn = (width * (n - t)) % LANES
                        moved = right_by(sums[n], turn) if turn else sums[n]
                        joint = jnp.where(lanes // width == n, moved, joint)
                    mixed[s][q + groups * t] = joint
        place = pl.ds(tile * LANES, LANES)
        for s in range(SECTIONS):
            turned = jnp.swapaxes(jnp.stack(mixed[s]), 0, 1)
            sections[s, :, :, place] = turned
            if s == SECTIONS - 1:
                next_voltage[:, :, place] = voltage[:, :, place] + turned


def local(voltage, capacity, node_class, via_sites, ball_sites, load_type, load_table):
    layers, block, wide = voltage.shape
    gx_count = lax.axis_size("gx")
    gy_count = lax.axis_size("gy")
    parts = lax.axis_size("section") * gx_count
    regions = parts // 2
    width = wide // regions
    margin = (LANES - width) // 2
    sizes = (parts, gx_count, gy_count, width, margin, wide * gy_count)
    rows = parts * block
    count = 4 * block + 1
    packs = -(-count // (LANES // margin))

    def vmem(*shape):
        return pltpu.VMEM(shape, jnp.float32)

    def levels(count, extra):
        return [vmem(count, rows // 2**m + extra, layers, LANES) for m in range(LEVELS)]

    mid = rows * margin // LANES if margin < BOTH_CYCLES else 1
    groups = block * width // LANES
    back = max(groups // 2, 1) + 2 * groups
    return pl.pallas_call(
        functools.partial(kernel, sizes, radau_tables()),
        out_shape=(
            jax.ShapeDtypeStruct((SECTIONS, layers, block, wide), jnp.float32),
            jax.ShapeDtypeStruct((layers, block, wide), jnp.float32),
        ),
        in_specs=[
            pl.BlockSpec(memory_space=pltpu.SMEM),
            *[pl.BlockSpec(memory_space=pltpu.VMEM)] * 6,
        ],
        out_specs=(
            pl.BlockSpec(memory_space=pltpu.VMEM),
            pl.BlockSpec(memory_space=pltpu.VMEM),
        ),
        scratch_shapes=[
            vmem(count, layers, wide),
            vmem(2, packs, layers, LANES),
            vmem(2, packs, layers, LANES),
            vmem(regions, count, layers, LANES),
            vmem(parts, count, layers, LANES),
            vmem(3, parts, block, LANES),
            *levels(10, 0),
            *levels(3, 1),
            *levels(3, 0),
            vmem(2, 3, mid, layers, LANES),
            vmem(2, 3, mid, layers, LANES),
            vmem(parts, back, layers, LANES),
            vmem(parts, back, layers, LANES),
            pltpu.SemaphoreType.DMA((2,)),
            pltpu.SemaphoreType.DMA((2,)),
            pltpu.SemaphoreType.DMA((regions,)),
            pltpu.SemaphoreType.DMA((regions,)),
            pltpu.SemaphoreType.DMA((regions,)),
            pltpu.SemaphoreType.DMA((regions,)),
            pltpu.SemaphoreType.DMA((2,)),
            pltpu.SemaphoreType.DMA((2,)),
            pltpu.SemaphoreType.DMA((parts,)),
            pltpu.SemaphoreType.DMA((parts,)),
            pltpu.SemaphoreType.DMA,
        ],
        compiler_params=pltpu.CompilerParams(
            collective_id=0, has_side_effects=True, vmem_limit_bytes=60 * 1024 * 1024
        ),
    )(load_table, voltage, capacity, node_class, via_sites, ball_sites, load_type)


def solution(mesh):
    return jax.shard_map(
        local,
        mesh=mesh,
        in_specs=(
            P(None, row_axes, "gy"),
            P(None, row_axes, "gy"),
            P(None, row_axes, "gy"),
            P(None, row_axes, "gy"),
            P(row_axes, "gy"),
            P(row_axes, "gy"),
            P(),
        ),
        out_specs=(P(None, None, row_axes, "gy"), P(None, row_axes, "gy")),
        check_vma=False,
    )
```
